128 devices in a mesh: seq: 32 (over y, x, core), head: 4 (over z).
Axes of the slice: x: 4, y: 4, z: 4, core: 2. Of those that a mesh axis runs over, the one named last changes fastest.
Arguments:
- tokens: bfloat16 [2, 32768, 2048], P(None, ('seq', 'head')), may hold values from -6 to 6
- norm_gain: float32 [2048], replicated, may hold values from 0.25 to 1.75
- projection: bfloat16 [2048, 6144], P(None, 'head'), may hold values from -0.125 to 0.125
- level_table: float32 [16, 16, 18], P(None, 'head'), may hold values from 0.05 to 1
- level_index: int32 [2, 32768], P(None, 'seq'), may hold values from 0 to 15
- lengths: int32 [2], replicated, may hold values from 16384 to 32768, as said below
Outputs:
- attended: bfloat16 [2, 32768, 2048], P(None, 'seq', 'head')
The draws below stay inside these ranges and needn't reach their ends.
Inputs may be any that keep to these rules, and one draw needn't show every extreme that they name: The first sequence is always whole: lengths[0] = 32768.
All inputs are finite; a program needn't handle non-finite values.
Results may differ from the reference program's by a relative error of at most 0.0097.
Values may be sent and summed in bfloat16 or wider, within the bound.
No kernel may reach another device: no remote copies, remote signals or barrier semaphores. Data moves between devices by JAX's collectives and lax.ppermute only.
A program may use at most 128 MiB of HBM per device.

```python
import math
import jax
import jax.numpy as jnp
from jax import lax

D = 2048
H = 16
DH = 128
SEQS = 2
SPAN = 512
TABLES = 16
LEVELS = 18
LEN = 32768


def draw_lengths(key, part):
    others = jax.random.randint(jax.random.fold_in(key, 7), (SEQS - 1,), LEN // 2, LEN + 1, dtype=jnp.int32)
    return jnp.concatenate([jnp.full((1,), LEN, jnp.int32), others])


def plant(values, key, least, largest):
    spot = [jax.random.randint(jax.random.fold_in(key, axis), (), 0, length) for axis, length in enumerate(values.shape)]
    main_axis = values.shape.index(max(values.shape))
    next_to = spot[:main_axis] + [(spot[main_axis] + 1) % values.shape[main_axis]] + spot[main_axis + 1:]
    return values.at[tuple(spot)].set(least).at[tuple(next_to)].set(largest)


def block_levels(stream_key, dims, pieces, least, largest):
    loudness = 1.0
    for axis_at, blocks in pieces:
        draws = jax.random.uniform(jax.random.fold_in(jax.random.fold_in(stream_key, 6), axis_at), (blocks,), jnp.float32, least / len(pieces), largest / len(pieces))
        loudness = loudness * jnp.repeat(jnp.exp(draws), dims[axis_at] // blocks).reshape((-1,) + (1,) * (len(dims) - 1 - axis_at))
    return loudness


def normal_values(own_key, extent, scale, most, cuts=(), held_as=jnp.bfloat16):
    drawn = jax.random.normal(own_key, extent, jnp.float32) * scale
    if len(cuts) > 0:
        drawn = block_levels(own_key, extent, cuts, -0.22, 0.18) * drawn
    return jnp.clip(drawn, min=-most, max=most).astype(held_as)


def setup_inputs(seed: int = 0) -> dict:
    splits = jax.random.split(jax.random.key(seed), 7)
    tokens = normal_values(splits[0], (SEQS, LEN, D), 1.0, 6.0, ((1, 128),))
    norm_gain = jnp.clip(1.0 + 0.15 * jax.random.normal(splits[1], (D,), jnp.float32), 0.25, 1.75)
    projection = normal_values(splits[2], (D, 3 * D), D ** -0.5, 0.125, ((1, 4),))
    level_table = jnp.clip(jnp.exp(math.log(1.0) - 2.9957323 * jax.random.uniform(splits[3], (TABLES, H, LEVELS), jnp.float32) ** block_levels(splits[3], (TABLES, H, LEVELS), ((1, 4),), -0.2, 0.2)), 0.05, 1.0)
    level_index = plant(jax.random.randint(splits[4], (SEQS, LEN), 0, TABLES), jax.random.fold_in(splits[4], 1), 0, TABLES - 1).astype(jnp.int32)
    lengths = draw_lengths(jax.random.fold_in(splits[6], 71), 0)
    return dict(tokens=tokens, norm_gain=norm_gain, projection=projection, level_table=level_table, level_index=level_index, lengths=lengths)


def digit_count(values, limit):
    counted = jnp.zeros(values.shape, jnp.int32)
    for shift in range(limit):
        counted = counted + (values >= 1 << shift).astype(jnp.int32)
    return counted

def reference(tokens, norm_gain, projection, level_table, level_index, lengths):
    widened = tokens.astype(jnp.float32)
    normed = (widened * lax.rsqrt(lax.optimization_barrier(jnp.mean(widened * widened, -1, keepdims=True)) + 1e-06) * norm_gain).astype(jnp.bfloat16)

    def project_one(rows_seq):
        return jnp.dot(rows_seq, projection, preferred_element_type=jnp.float32).astype(jnp.bfloat16)
    projected = lax.map(project_one, normed).reshape(SEQS, LEN, H, 3, DH)
    projected = projected.transpose(2, 3, 0, 1, 4)
    weights = level_table[level_index].transpose(2, 0, 1, 3)
    span_total = LEN // SPAN
    span_bits = span_total.bit_length() - 1
    lchunk = SPAN.bit_length() - 1
    positions = jnp.arange(SPAN, dtype=jnp.int32)
    level_grid = digit_count(jnp.bitwise_xor(positions[:, None], positions[None, :]), lchunk + 1)
    causal = (positions[:, None] >= positions[None, :]).astype(jnp.float32)
    span_ids = jnp.arange(span_total, dtype=jnp.int32)
    span_dist = digit_count(jnp.bitwise_xor(span_ids[:, None], span_ids[None, :]), span_bits + 1)
    span_earlier = span_ids[None, :] < span_ids[:, None]
    span_mask = jnp.stack([((span_dist == step + 1) & span_earlier).astype(jnp.float32) for step in range(span_bits)])
    highest = lax.Precision.HIGHEST

    def one_head(inputs):
        head_qkv, head_weights = inputs
        queries = head_qkv[0].reshape(SEQS, span_total, SPAN, DH).astype(jnp.float32)
        keys_here = head_qkv[1].reshape(SEQS, span_total, SPAN, DH).astype(jnp.float32)
        values_here = head_qkv[2].reshape(SEQS, span_total, SPAN, DH).astype(jnp.float32)
        level_weight = head_weights.reshape(SEQS, span_total, SPAN, LEVELS)
        scores = jnp.einsum('sctd,scud->sctu', queries, keys_here, precision=highest)
        grid = jnp.zeros(scores.shape, jnp.float32)
        for level_step in range(lchunk + 1):
            grid = grid + level_weight[..., level_step][..., None] * (level_grid == level_step).astype(jnp.float32)
        weighted = (scores * grid * causal).astype(jnp.bfloat16).astype(jnp.float32)
        near_part = jnp.einsum('sctu,scue->scte', weighted, values_here, precision=highest)
        states = jnp.einsum('sctd,scte->scde', keys_here, values_here, precision=highest)
        far_part = jnp.zeros(near_part.shape, jnp.float32)
        for level_step in range(span_bits):
            bucket = jnp.einsum('cb,sbde->scde', span_mask[level_step], states, precision=highest)
            bucket = bucket.astype(jnp.bfloat16).astype(jnp.float32)
            readout = jnp.einsum('sctd,scde->scte', queries, bucket, precision=highest)
            far_part = far_part + level_weight[..., lchunk + 1 + level_step][..., None] * readout
        output = near_part + far_part
        output = output * lax.rsqrt(lax.optimization_barrier(jnp.mean(output * output, -1, keepdims=True)) + 1e-06)
        return output.reshape(SEQS, LEN, DH)
    heads_out = lax.map(one_head, (projected, weights))
    attended = heads_out.transpose(1, 2, 0, 3).reshape(SEQS, LEN, D)
    valid = jnp.arange(LEN, dtype=jnp.int32)[None, :] < lengths[:, None]
    return jnp.where(valid[..., None], attended, 0.0).astype(jnp.bfloat16)
```

```python
import jax
import jax.numpy as jnp
from jax import lax
from jax.experimental import pallas as pl
from jax.experimental.pallas import tpu as pltpu
from jax.sharding import PartitionSpec as P


TILE = 128
LANES = 128
HEAD_LANES = 32
F32 = jnp.float32
BF16 = jnp.bfloat16


def near_tile(q, k, v, wt, base, differ, causal):
    scores = lax.dot_general(q, k, (((1,), (1,)), ((), ())), preferred_element_type=F32)
    grid = jnp.broadcast_to(wt[:, base : base + 1], (TILE, TILE))
    for level in range(1, 8):
        grid = jnp.where(
            differ >= 1 << (level - 1),
            jnp.broadcast_to(wt[:, base + level : base + level + 1], (TILE, TILE)),
            grid,
        )
    weighted = jnp.where(causal, scores * grid, 0.0).astype(BF16)
    return jnp.dot(weighted, v, preferred_element_type=F32)


def project_kernel(pieces, chunks, heads_step):
    rows_piece = [piece[1] for piece in pieces]

    def body(idx_ref, *refs):
        xs = refs[: len(pieces)]
        gain_ref, w_ref = refs[len(pieces) : len(pieces) + 2]
        wts = refs[len(pieces) + 2 : len(pieces) + 2 + chunks]
        q_ref, near_ref, state_ref, normed = refs[len(pieces) + 2 + chunks :]
        step = pl.program_id(0)

        @pl.when(step == 0)
        def _():
            at = 0
            for x_ref, (count, rows) in zip(xs, pieces):
                for i in range(count):
                    x = x_ref[i].astype(F32)
                    scale = lax.rsqrt(jnp.mean(x * x, -1, keepdims=True) + 1e-06)
                    normed[pl.ds(at, rows), :] = (x * scale * gain_ref[...]).astype(BF16)
                    at += rows

        row_at = lax.broadcasted_iota(jnp.int32, (TILE, TILE), 0)
        col_at = lax.broadcasted_iota(jnp.int32, (TILE, TILE), 1)
        differ = jnp.bitwise_xor(row_at, col_at)
        causal = col_at <= row_at
        for c in range(chunks):
            qkv = jnp.dot(
                normed[pl.ds(c * 2 * TILE, 2 * TILE), :], w_ref[...], preferred_element_type=F32
            ).astype(BF16)
            wt_all = wts[c][0, 0]
            for hh in range(heads_step):
                wt = wt_all[:, hh * HEAD_LANES : (hh + 1) * HEAD_LANES]
                if heads_step * 2 == LANES // HEAD_LANES:
                    other = wt_all[
                        :, (hh + heads_step) * HEAD_LANES : (hh + heads_step + 1) * HEAD_LANES
                    ]
                    wt = jnp.where(step == 0, wt, other)
                q = qkv[:, hh * 384 : hh * 384 + 128]
                k = qkv[:, hh * 384 + 128 : hh * 384 + 256]
                v = qkv[:, hh * 384 + 256 : hh * 384 + 384]
                states = []
                for t in range(2):
                    rows = slice(t * TILE, (t + 1) * TILE)
                    near = near_tile(q[rows], k[rows], v[rows], wt[rows], 0, differ, causal)
                    if t == 1:
                        readout = jnp.dot(
                            q[rows], states[0].astype(BF16), preferred_element_type=F32
                        )
                        near = near + wt[rows, 8:9] * readout
                    states.append(
                        lax.dot_general(
                            k[rows], v[rows], (((0,), (0,)), ((), ())), preferred_element_type=F32
                        )
                    )
                    near_ref[c, rows, hh * 128 : (hh + 1) * 128] = near
                q_ref[c, :, hh * 128 : (hh + 1) * 128] = q
                state_ref[c, hh] = states[0] + states[1]

    return body


def project(xs, seqs, places, gain, projection, wt):
    pieces = [(x.shape[0], x.shape[1]) for x in xs]
    chunks = len(seqs)
    width, cols = projection.shape
    heads = cols // 384
    heads_step = 2 if heads % 2 == 0 else 1
    steps = heads // heads_step
    rows = chunks * 2 * TILE
    wt_specs = [
        pl.BlockSpec((1, 1, 2 * TILE, LANES), lambda j, idx, s=s, i=i: (s, idx[i], 0, 0))
        for i, s in enumerate(seqs)
    ]
    return pl.pallas_call(
        project_kernel(pieces, chunks, heads_step),
        grid_spec=pltpu.PrefetchScalarGridSpec(
            num_scalar_prefetch=1,
            grid=(steps,),
            in_specs=[pl.BlockSpec(x.shape, lambda j, idx: (0, 0, 0)) for x in xs]
            + [
                pl.BlockSpec((1, width), lambda j, idx: (0, 0)),
                pl.BlockSpec((width, heads_step * 384), lambda j, idx: (0, j)),
            ]
            + wt_specs,
            out_specs=[
                pl.BlockSpec((chunks, 2 * TILE, heads_step * 128), lambda j, idx: (0, 0, j)),
                pl.BlockSpec((chunks, 2 * TILE, heads_step * 128), lambda j, idx: (0, 0, j)),
                pl.BlockSpec((chunks, heads_step, 128, 128), lambda j, idx: (0, j, 0, 0)),
            ],
            scratch_shapes=[pltpu.VMEM((rows, width), BF16)],
        ),
        out_shape=[
            jax.ShapeDtypeStruct((chunks, 2 * TILE, heads * 128), BF16),
            jax.ShapeDtypeStruct((chunks, 2 * TILE, heads * 128), F32),
            jax.ShapeDtypeStruct((chunks, heads, 128, 128), F32),
        ],
        cost_estimate=pl.CostEstimate(
            flops=2 * rows * width * cols, transcendentals=rows, bytes_accessed=width * cols * 2
        ),
        name="project_near",
    )(jnp.stack(places).astype(jnp.int32), *xs, gain.reshape(1, width), projection, *([wt] * chunks))


def far_kernel(seq_levels):
    before = [1, 3, 0, 2]

    def body(idx_ref, flag_ref, limit_ref, *refs):
        qs = refs[0:4]
        nears = refs[4:8]
        states = refs[8:12]
        buckets = refs[12 : 12 + seq_levels]
        wt_ref = refs[12 + seq_levels]
        out_ref = refs[-1]
        head = pl.program_id(0)
        st = [states[r][0, 0] for r in range(4)]
        far_buckets = [
            (buckets[j][0].astype(F32) * flag_ref[16 + j]).astype(BF16) for j in range(seq_levels)
        ]
        for r in range(4):
            place = idx_ref[r]
            q = qs[r][0]
            wt_all = wt_ref[0, place]
            wt = wt_all[:, 0:HEAD_LANES]
            for hh in range(1, LANES // HEAD_LANES):
                wt = jnp.where(head == hh, wt_all[:, hh * HEAD_LANES : (hh + 1) * HEAD_LANES], wt)
            level9 = (st[before[r]] * flag_ref[r]).astype(BF16)
            level10 = sum(
                [st[o] * flag_ref[24 + r * 4 + o] for o in range(4) if o != r]
            ).astype(BF16)
            mats = [level9, level10] + far_buckets
            acc = nears[r][0]
            for j, mat in enumerate(mats):
                acc = acc + wt[:, 9 + j : 10 + j] * jnp.dot(q, mat, preferred_element_type=F32)
            acc = acc * lax.rsqrt(jnp.mean(acc * acc, -1, keepdims=True) + 1e-06)
            position = place * (2 * TILE) + lax.broadcasted_iota(jnp.int32, (2 * TILE, 128), 0)
            out_ref[0, place] = jnp.where(position < limit_ref[0], acc, 0.0).astype(BF16)

    return body


def far(places, flags, limit, qs, nears, states, picks, buckets, wt, seq, heads, out_prev, seqs):
    seq_levels = len(buckets)
    in_specs = (
        [pl.BlockSpec((1, 2 * TILE, 128), lambda h, *_, c=c: (c, 0, h)) for c in picks]
        + [pl.BlockSpec((1, 2 * TILE, 128), lambda h, *_, c=c: (c, 0, h)) for c in picks]
        + [pl.BlockSpec((1, 1, 128, 128), lambda h, *_, c=c: (c, h, 0, 0)) for c in picks]
        + [pl.BlockSpec((1, 128, 128), lambda h, *_: (h, 0, 0)) for _ in buckets]
        + [pl.BlockSpec((1, 4, 2 * TILE, LANES), lambda h, *_: (seq, 0, 0, 0))]
    )
    args = [*qs, *nears, *states, *buckets, wt]
    aliases = {}
    if out_prev is not None:
        in_specs.append(pl.BlockSpec(memory_space=pl.ANY))
        args.append(out_prev)
        aliases = {3 + len(args) - 1: 0}
    return pl.pallas_call(
        far_kernel(seq_levels),
        grid_spec=pltpu.PrefetchScalarGridSpec(
            num_scalar_prefetch=3,
            grid=(heads,),
            in_specs=in_specs,
            out_specs=pl.BlockSpec((1, 4, 2 * TILE, 128), lambda h, *_: (seq, 0, 0, h)),
        ),
        out_shape=jax.ShapeDtypeStruct((seqs, 4, 2 * TILE, heads * 128), BF16),
        input_output_aliases=aliases,
        cost_estimate=pl.CostEstimate(
            flops=2 * 1024 * 128 * 128 * heads * 7, transcendentals=0, bytes_accessed=5 << 20
        ),
        name="far_part",
    )(places, flags, limit, *args)


def on_device(tokens, norm_gain, projection, level_table, level_index, lengths):
    seqs, row_count, width = tokens.shape
    tables, heads, level_total = level_table.shape
    groups = lax.axis_size("head")
    seq_size = lax.axis_size("seq")
    seq_bits = seq_size.bit_length() - 1
    z = lax.axis_index("head")
    own_index = lax.axis_index("seq")
    half = row_count // 2
    up = [(i, (i + 1) % groups) for i in range(groups)]
    down = [(i, (i - 1) % groups) for i in range(groups)]

    onehot = (level_index[..., None] == jnp.arange(tables, dtype=jnp.int32)).astype(F32)
    table = jnp.pad(level_table, ((0, 0), (0, 0), (0, HEAD_LANES - level_total)))
    wt = jnp.einsum(
        "stg,gl->stl", onehot, table.reshape(tables, heads * HEAD_LANES), precision=lax.Precision.HIGHEST
    ).reshape(seqs, groups, row_count, heads * HEAD_LANES)

    place = [z, (z + 3) % 4, (z + 1) % 4, (z + 2) % 4]
    places = jnp.stack(place).astype(jnp.int32)

    got = []
    for s in range(seqs):
        mine = tokens[s : s + 1]
        a = lax.ppermute(mine, "head", up)
        b = lax.ppermute(mine, "head", down)
        c = lax.ppermute(a[:, :half], "head", up)
        d = lax.ppermute(b[:, half:], "head", down)
        got.append((a, b, c, d))

    own = project([tokens], [0, 1], [place[0], place[0]], norm_gain, projection, wt)
    parts = []
    for s in range(seqs):
        a, b, c, d = got[s]
        ab = project([a, b], [s, s], [place[1], place[2]], norm_gain, projection, wt)
        cd = project([c, d], [s], [place[3]], norm_gain, projection, wt)
        parts.append((ab, cd))

    odd = [(p % 2).astype(F32) for p in place]
    flags = [jnp.float32(0)] * 40
    for r in range(4):
        flags[r] = odd[r]
        for o in range(4):
            flags[24 + r * 4 + o] = ((place[r] >= 2) & (place[o] < 2)).astype(F32)
    for j in range(seq_bits):
        flags[16 + j] = ((own_index >> j) & 1).astype(F32)
    flags = jnp.stack(flags)

    out = None
    for s in range(seqs):
        ab, cd = parts[s]
        total = own[2][s] + ab[2][0] + ab[2][1] + cd[2][0]
        buckets = []
        for j in range(seq_bits):
            pairs = [(i, i ^ (1 << j)) for i in range(seq_size)]
            received = lax.ppermute(total.astype(BF16), "seq", pairs)
            buckets.append(received)
            total = total + received.astype(F32)
        limit = (lengths[s] - own_index * (row_count * groups)).reshape(1).astype(jnp.int32)
        out = far(
            places,
            flags,
            limit,
            [own[0], ab[0], ab[0], cd[0]],
            [own[1], ab[1], ab[1], cd[1]],
            [own[2], ab[2], ab[2], cd[2]],
            [s, 0, 1, 0],
            buckets,
            wt,
            s,
            heads,
            out,
            seqs,
        )
    return out.reshape(seqs, row_count * groups, heads * 128)


def solution(mesh):
    in_specs = (
        P(None, ("seq", "head"), None),
        P(),
        P(None, "head"),
        P(None, "head", None),
        P(None, "seq"),
        P(),
    )
    out_specs = P(None, "seq", "head")
    return jax.shard_map(
        on_device, mesh=mesh, in_specs=in_specs, out_specs=out_specs, check_vma=False
    )
```

```python
import jax
import jax.numpy as jnp
from jax import lax
from jax.experimental import pallas as pl
from jax.experimental.pallas import tpu as pltpu
from jax.sharding import PartitionSpec as P


TILE = 128
ROWS = 2 * TILE
F32 = jnp.float32
BF16 = jnp.bfloat16
NT = (((1,), (1,)), ((), ()))


def in_vmem(value):
    return pltpu.with_memory_space_constraint(value, pltpu.VMEM)


def fold_kernel(gain_ref, w_ref, out_ref):
    for at in range(0, w_ref.shape[0], TILE):
        column = jnp.broadcast_to(gain_ref[:, at : at + TILE], (TILE, TILE)).T
        for lane in range(0, w_ref.shape[1], TILE):
            part = w_ref[at : at + TILE, lane : lane + TILE].astype(F32) * column
            out_ref[at : at + TILE, lane : lane + TILE] = part.astype(BF16)


def fold_gain(gain, projection):
    width, cols = projection.shape
    return pl.pallas_call(
        fold_kernel,
        grid=(width // ROWS,),
        in_specs=[
            pl.BlockSpec((1, ROWS), lambda i: (0, i)),
            pl.BlockSpec((ROWS, cols), lambda i: (i, 0)),
        ],
        out_specs=pl.BlockSpec((ROWS, cols), lambda i: (i, 0)),
        out_shape=pltpu.VMEM((width, cols), BF16),
        compiler_params=pltpu.CompilerParams(vmem_limit_bytes=8 << 20),
        name="fold_gain",
    )(gain.reshape(1, width), pltpu.with_memory_space_constraint(projection, pltpu.HBM))


def place_of(relative):
    return (lax.axis_index("head") + (0, 3, 1, 2)[relative]) % 4


def project_kernel(pieces, relatives, heads_step, level_rows):
    cols = heads_step * 384
    chunks = len(relatives)

    def body(*refs):
        xs = refs[: len(pieces)]
        w_ref, wt_ref = refs[len(pieces) : len(pieces) + 2]
        q_ref, near_ref, state_ref, wt_out, held, scales = refs[len(pieces) + 2 :]
        step = pl.program_id(0)

        @pl.when(step == 0)
        def _():
            at = 0
            sums = []
            for x_ref, (count, rows) in zip(xs, pieces):
                for i in range(count):
                    x = x_ref[i]
                    held[pl.ds(at, rows), :] = x
                    at += rows
                    total = jnp.zeros((rows, TILE), F32)
                    for lane in range(0, x.shape[1], TILE):
                        part = x[:, lane : lane + TILE].astype(F32)
                        total = total + part * part
                    sums.append(total)
            sums = jnp.concatenate(sums, axis=0)
            ones = jnp.full((8, TILE), 1.0, F32)
            for c in range(chunks):
                mean = lax.dot_general(
                    ones,
                    sums[c * ROWS : (c + 1) * ROWS],
                    NT,
                    precision=lax.Precision.HIGHEST,
                    preferred_element_type=F32,
                ) * (1.0 / held.shape[1])
                scales[c] = lax.rsqrt(mean + 1e-06)

        source = lax.broadcasted_iota(jnp.int32, (TILE, TILE), 0)
        target = lax.broadcasted_iota(jnp.int32, (TILE, TILE), 1)
        differ = jnp.bitwise_xor(source, target)
        causal = source <= target
        zeros = jnp.zeros((TILE, TILE), BF16)
        every = [(c, hh) for c in range(chunks) for hh in range(heads_step)]
        qkv = jnp.dot(held[...], w_ref[:, pl.ds(pl.multiple_of(step * cols, cols), cols)], preferred_element_type=F32)
        q, k, v, scores = {}, {}, {}, {}
        for c in range(chunks):
            scale = scales[c, 0:1, :]
            wt_out[c] = wt_ref[0, place_of(relatives[c])] * scale
            rows = slice(c * ROWS, (c + 1) * ROWS)
            for hh in range(heads_step):
                at = hh * 384
                q[c, hh] = qkv[rows, at : at + 128].T.astype(BF16)
                k[c, hh] = qkv[rows, at + 128 : at + 256].astype(BF16)
                v[c, hh] = (qkv[rows, at + 256 : at + 384].T * (scale * scale)).astype(BF16)
                q_ref[c, hh * 128 : (hh + 1) * 128, :] = q[c, hh]
        for i in every:
            scores[i] = jnp.dot(k[i], q[i], preferred_element_type=F32)
            state_ref[i[0], i[1]] = jnp.dot(v[i], k[i], preferred_element_type=F32)
        for c, hh in every:
            base = hh * level_rows
            blocks = []
            for t in range(2):
                lanes = slice(t * TILE, (t + 1) * TILE)
                grid = wt_out[c, base : base + 1, lanes]
                for level in range(1, 8):
                    row = wt_out[c, base + level : base + level + 1, lanes]
                    grid = jnp.where(differ >= 1 << (level - 1), row, grid)
                grid = jnp.where(causal, grid, 0.0)
                blocks.append((scores[c, hh][lanes, lanes] * grid).astype(BF16))
            row = wt_out[c, base + 8 : base + 9, TILE:]
            cross = (scores[c, hh][:TILE, TILE:] * row).astype(BF16)
            weighted = jnp.concatenate(
                [
                    jnp.concatenate([blocks[0], cross], axis=1),
                    jnp.concatenate([zeros, blocks[1]], axis=1),
                ],
                axis=0,
            )
            near = jnp.dot(v[c, hh], weighted, preferred_element_type=F32)
            near_ref[c, hh * 128 : (hh + 1) * 128, :] = near

    return body


def project(xs, seq, relatives, weight, wt, pick=0):
    pieces = [(1, x.shape[1]) for x in xs]
    chunks = len(relatives)
    width, cols = weight.shape
    heads = cols // 384
    heads_step = 2 if heads % 2 == 0 else 1
    level_rows = wt.shape[2] // heads
    rows = chunks * ROWS
    return pl.pallas_call(
        project_kernel(pieces, relatives, heads_step, level_rows),
        grid=(heads // heads_step,),
        in_specs=[pl.BlockSpec((1,) + x.shape[1:], lambda j: (pick, 0, 0)) for x in xs]
        + [pl.BlockSpec(memory_space=pltpu.VMEM)]
        + [pl.BlockSpec((1, 4, heads_step * level_rows, ROWS), lambda j: (seq, 0, j, 0))],
        out_specs=[
            pl.BlockSpec((chunks, heads_step * 128, ROWS), lambda j: (0, j, 0)),
            pl.BlockSpec((chunks, heads_step * 128, ROWS), lambda j: (0, j, 0)),
            pl.BlockSpec((chunks, heads_step, 128, 128), lambda j: (0, j, 0, 0)),
            pl.BlockSpec((chunks, heads_step * level_rows, ROWS), lambda j: (0, j, 0)),
        ],
        scratch_shapes=[pltpu.VMEM((rows, width), BF16), pltpu.VMEM((chunks, 8, ROWS), F32)],
        out_shape=[
            pltpu.VMEM((chunks, heads * 128, ROWS), BF16),
            pltpu.VMEM((chunks, heads * 128, ROWS), F32),
            pltpu.VMEM((chunks, heads, 128, 128), F32),
            pltpu.VMEM((chunks, heads * level_rows, ROWS), F32),
        ],
        cost_estimate=pl.CostEstimate(
            flops=2 * rows * width * cols, transcendentals=rows, bytes_accessed=width * cols * 2
        ),
        compiler_params=pltpu.CompilerParams(vmem_limit_bytes=16 << 20),
        name="project_near",
    )(*xs, in_vmem(weight), wt)


def far_kernel(seq, half_heads):
    before = [1, 3, 0, 2]

    def body(lengths_ref, *refs):
        qs, nears, states, wts = refs[0:4], refs[4:8], refs[8:12], refs[12:16]
        core_ref, mine_ref, other_ref = refs[16:19]
        out_ref = refs[-1]
        core = lax.axis_index("seq") % 2
        places = [place_of(r) for r in range(4)]
        limit = lengths_ref[seq] - lax.axis_index("seq") * (4 * ROWS)
        st = [states[r][0, 0] for r in range(4)]
        is_mine = pl.program_id(0) // half_heads == core
        level11 = (core_ref[0].astype(F32) * core.astype(F32)).astype(BF16)
        levels = mine_ref.shape[0]
        picked = [jnp.where(is_mine, mine_ref[j, 0], other_ref[j, 0]) for j in range(levels)]
        far_buckets = jnp.concatenate([level11] + picked, axis=1)
        at = lax.broadcasted_iota(jnp.int32, (1, ROWS), 1)
        for r in range(4):
            place = places[r]
            q = qs[r][0]
            level9 = st[before[r]] * (place % 2).astype(F32)
            upper = (place // 2).astype(F32)
            level10 = sum(
                [st[o] * (upper * (1 - places[o] // 2).astype(F32)) for o in range(4) if o != r]
            )
            mats = jnp.concatenate(
                [level9.astype(BF16), level10.astype(BF16), far_buckets], axis=1
            )
            q16 = q.reshape(8, 16, ROWS)
            scaled = []
            for j in range(3 + levels):
                row = jnp.broadcast_to(wts[r][0, 9 + j : 10 + j, :], (16, ROWS)).astype(BF16)
                scaled.append((q16 * row[None]).reshape(128, ROWS))
            scaled = jnp.concatenate(scaled, axis=0)
            acc = nears[r][0] + jnp.dot(mats, scaled, preferred_element_type=F32)
            scale = lax.rsqrt(jnp.mean(acc * acc, 0, keepdims=True) + 1e-06)
            valid = place * ROWS + at < limit
            acc = jnp.where(valid, acc * scale, 0.0)
            out_ref[0, place] = acc.T.astype(BF16)

    return body


def far(lengths, chunks, core_bucket, mine, other, seq, out_prev, seqs):
    heads = core_bucket.shape[0]
    levels, half_heads = mine.shape[:2]
    level_rows = chunks[0][0][3].shape[1] // heads
    picks = [c for _, c in chunks]
    in_specs = (
        [pl.BlockSpec(memory_space=pltpu.SMEM)]
        + [pl.BlockSpec((1, 128, ROWS), lambda h, c=c: (c, h, 0)) for c in picks]
        + [pl.BlockSpec((1, 128, ROWS), lambda h, c=c: (c, h, 0)) for c in picks]
        + [pl.BlockSpec((1, 1, 128, 128), lambda h, c=c: (c, h, 0, 0)) for c in picks]
        + [pl.BlockSpec((1, level_rows, ROWS), lambda h, c=c: (c, h, 0)) for c in picks]
        + [pl.BlockSpec((1, 128, 128), lambda h: (h, 0, 0))]
        + [pl.BlockSpec((levels, 1, 128, 128), lambda h: (0, h % half_heads, 0, 0))] * 2
    )
    args = [lengths] + [in_vmem(call[i]) for i in range(4) for call, _ in chunks]
    args += [core_bucket, mine, other]
    aliases = {}
    if out_prev is not None:
        in_specs.append(pl.BlockSpec(memory_space=pl.ANY))
        args.append(out_prev)
        aliases = {len(args) - 1: 0}
    return pl.pallas_call(
        far_kernel(seq, half_heads),
        grid=(heads,),
        in_specs=in_specs,
        out_specs=pl.BlockSpec((1, 4, ROWS, 128), lambda h: (seq, 0, 0, h)),
        out_shape=jax.ShapeDtypeStruct((seqs, 4, ROWS, heads * 128), BF16),
        input_output_aliases=aliases,
        cost_estimate=pl.CostEstimate(
            flops=2 * 1024 * 128 * 128 * heads * 7, transcendentals=0, bytes_accessed=5 << 20
        ),
        compiler_params=pltpu.CompilerParams(vmem_limit_bytes=8 << 20),
        name="far_part",
    )(*args)


def small_call(body, outs, *args):
    return pl.pallas_call(
        body,
        in_specs=[pl.BlockSpec(memory_space=pltpu.VMEM)] * len(args),
        out_specs=[pl.BlockSpec(memory_space=pltpu.VMEM)] * len(outs),
        out_shape=[jax.ShapeDtypeStruct(shape, dtype) for shape, dtype in outs],
        compiler_params=pltpu.CompilerParams(vmem_limit_bytes=4 << 20),
    )(*args)


def seq_bit(j):
    return (lax.axis_index("seq") // (1 << j)) % 2


def total_kernel(own_ref, ab_ref, cd_ref, total_ref, sent_ref):
    total = own_ref[0] + ab_ref[0] + ab_ref[1] + cd_ref[0]
    total_ref[...] = total
    sent_ref[...] = total.astype(BF16)


def core_kernel(total_ref, received_ref, part_ref, sent_ref):
    half = part_ref.shape[0]
    heads = pl.ds(seq_bit(0) * half, half)
    part = total_ref[heads] + received_ref[heads].astype(F32)
    part_ref[...] = part
    sent_ref[...] = part.astype(BF16)


def stage_kernel(low, last):
    def body(part_ref, one_ref, two_ref, three_ref, *refs):
        one, two, three = [r[...].astype(F32) for r in (one_ref, two_ref, three_ref)]
        near_level = (one * seq_bit(low).astype(F32)).astype(BF16)
        far_level = ((two + three) * seq_bit(low + 1).astype(F32)).astype(BF16)
        if last:
            before_ref, mine_ref = refs
            count = before_ref.shape[0]
            mine_ref[0:count] = before_ref[...]
            mine_ref[count] = near_level
            mine_ref[count + 1] = far_level
        else:
            mine_ref, next_ref, sent_ref = refs
            mine_ref[0] = near_level
            mine_ref[1] = far_level
            part = part_ref[...] + (one + (two + three))
            next_ref[...] = part
            sent_ref[...] = part.astype(BF16)

    return body


def exchange(own, ab, cd):
    size = lax.axis_size("seq")
    heads = own.shape[1]
    whole, half = (heads, 128, 128), (heads // 2, 128, 128)

    def swap(value, mask):
        return lax.ppermute(value, "seq", [(i, i ^ mask) for i in range(size)])

    total, sent = small_call(
        total_kernel, [(whole, F32), (whole, BF16)], *map(in_vmem, (own, ab, cd))
    )
    core_bucket = swap(sent, 1)
    part, sent = small_call(core_kernel, [(half, F32), (half, BF16)], total, core_bucket)
    heard = [swap(sent, mask << 1) for mask in (1, 2, 3)]
    levels, part, sent = small_call(
        stage_kernel(1, False), [((2,) + half, BF16), (half, F32), (half, BF16)], part, *heard
    )
    heard = [swap(sent, mask << 3) for mask in (1, 2, 3)]
    (mine,) = small_call(stage_kernel(3, True), [((4,) + half, BF16)], part, *heard, levels)
    return core_bucket, mine, swap(mine, 1)


def on_device(tokens, norm_gain, projection, level_table, level_index, lengths):
    seqs, row_count, _ = tokens.shape
    tables, heads, level_total = level_table.shape
    groups = lax.axis_size("head")
    half = row_count // 2
    up = [(i, (i + 1) % groups) for i in range(groups)]
    down = [(i, (i - 1) % groups) for i in range(groups)]

    got = []
    held = tokens
    for s in range(seqs):
        low, high = held[s : s + 1, :half], held[s : s + 1, half:]
        a_low = lax.ppermute(low, "head", up)
        b_high = lax.ppermute(high, "head", down)
        a_high = lax.ppermute(high, "head", up)
        b_low = lax.ppermute(low, "head", down)
        if s + 1 < seqs:
            held, a_low, b_high = lax.optimization_barrier((tokens, a_low, b_high))
        c = lax.ppermute(a_low, "head", up)
        d = lax.ppermute(b_high, "head", down)
        got.append(([a_low, a_high, b_low, b_high], [c, d]))

    level_rows = -(-level_total // 8) * 8
    onehot = (level_index[..., None] == jnp.arange(tables, dtype=jnp.int32)).astype(F32)
    table = jnp.pad(level_table, ((0, 0), (0, 0), (0, level_rows - level_total)))
    wt = jnp.einsum(
        "gm,szrg->szmr",
        table.reshape(tables, heads * level_rows),
        onehot.reshape(seqs, groups, row_count, tables),
        precision=lax.Precision.HIGHEST,
    )

    weight = fold_gain(norm_gain, projection)

    own = []
    for s in range(seqs):
        own.append(project([tokens], s, [0], weight, wt, s))
    parts = []
    for s in range(seqs):
        ab = project(got[s][0], s, [1, 2], weight, wt)
        cd = project(got[s][1], s, [3], weight, wt)
        parts.append((ab, cd))

    out = None
    for s in range(seqs):
        ab, cd = parts[s]
        core_bucket, mine, other = exchange(own[s][2], ab[2], cd[2])
        chunks = [(own[s], 0), (ab, 0), (ab, 1), (cd, 0)]
        out = far(lengths, chunks, core_bucket, mine, other, s, out, seqs)
    return out.reshape(seqs, row_count * groups, heads * 128)


def solution(mesh):
    in_specs = (
        P(None, ("seq", "head"), None),
        P(),
        P(None, "head"),
        P(None, "head", None),
        P(None, "seq"),
        P(),
    )
    out_specs = P(None, "seq", "head")

    return jax.shard_map(on_device, mesh=mesh, in_specs=in_specs, out_specs=out_specs, check_vma=False)
```

```python
import jax
import jax.numpy as jnp
from jax import lax
from jax.experimental import pallas as pl
from jax.experimental.pallas import tpu as pltpu
from jax.sharding import PartitionSpec as P


TILE = 128
ROWS = 2 * TILE
F32 = jnp.float32
BF16 = jnp.bfloat16
NT = (((1,), (1,)), ((), ()))


def in_vmem(value):
    return pltpu.with_memory_space_constraint(value, pltpu.VMEM)


def fold_kernel(gain_ref, w_ref, out_ref):
    heads = w_ref.shape[1] // (3 * TILE)
    for at in range(0, w_ref.shape[0], TILE):
        column = jnp.broadcast_to(gain_ref[:, at : at + TILE], (TILE, TILE)).T
        for lane in range(0, w_ref.shape[1], TILE):
            part = w_ref[at : at + TILE, lane : lane + TILE].astype(F32) * column
            head, which = divmod(lane // TILE, 3)
            to = head * TILE if which == 0 else heads * TILE + head * 2 * TILE + (which - 1) * TILE
            out_ref[at : at + TILE, to : to + TILE] = part.astype(BF16)


def fold_gain(gain, projection):
    width, cols = projection.shape
    return pl.pallas_call(
        fold_kernel,
        grid=(width // ROWS,),
        in_specs=[
            pl.BlockSpec((1, ROWS), lambda i: (0, i)),
            pl.BlockSpec((ROWS, cols), lambda i: (i, 0)),
        ],
        out_specs=pl.BlockSpec((ROWS, cols), lambda i: (i, 0)),
        out_shape=pltpu.VMEM((width, cols), BF16),
        compiler_params=pltpu.CompilerParams(vmem_limit_bytes=8 << 20),
        name="fold_gain",
    )(gain.reshape(1, width), pltpu.with_memory_space_constraint(projection, pltpu.HBM))


def place_of(relative):
    return (lax.axis_index("head") + (0, 3, 1, 2)[relative]) % 4


def row_scales(xs, pick, scales):
    sums = []
    for x_ref in xs:
        total = jnp.zeros((x_ref.shape[1], TILE), F32)
        for lane in range(0, x_ref.shape[2], TILE):
            part = x_ref[pick, :, lane : lane + TILE].astype(F32)
            total = total + part * part
        sums.append(total)
    sums = jnp.concatenate(sums, axis=0)
    ones = jnp.full((8, TILE), 1.0, F32)
    for c in range(scales.shape[0]):
        mean = lax.dot_general(
            ones,
            sums[c * ROWS : (c + 1) * ROWS],
            NT,
            precision=lax.Precision.HIGHEST,
            preferred_element_type=F32,
        ) * (1.0 / xs[0].shape[2])
        scales[c] = lax.rsqrt(mean + 1e-06)


def columns(w_ref, start, count):
    return w_ref[:, pl.ds(pl.multiple_of(start, TILE), count)]


def split_keys(kv, scale, rows, hh):
    at = hh * 256
    k = kv[rows, at : at + 128].astype(BF16)
    v = (kv[rows, at + 128 : at + 256].T * (scale * scale)).astype(BF16)
    return k, v


def near_parts(q, k, v, wt_out, near_ref, step, heads_step):
    source = lax.broadcasted_iota(jnp.int32, (TILE, TILE), 0)
    target = lax.broadcasted_iota(jnp.int32, (TILE, TILE), 1)
    differ = jnp.bitwise_xor(source, target)
    causal = source <= target
    zeros = jnp.zeros((TILE, TILE), BF16)
    scores = {i: jnp.dot(k[i], q[i], preferred_element_type=F32) for i in q}
    for c, hh in q:
        head = step * heads_step + hh
        blocks = []
        for t in range(2):
            lanes = slice(t * TILE, (t + 1) * TILE)
            grid = wt_out[c, head, 0:1, lanes]
            for level in range(1, 8):
                row = wt_out[c, head, level : level + 1, lanes]
                grid = jnp.where(differ >= 1 << (level - 1), row, grid)
            grid = jnp.where(causal, grid, 0.0)
            blocks.append((scores[c, hh][lanes, lanes] * grid).astype(BF16))
        row = wt_out[c, head, 8:9, TILE:]
        cross = (scores[c, hh][:TILE, TILE:] * row).astype(BF16)
        weighted = jnp.concatenate(
            [
                jnp.concatenate([blocks[0], cross], axis=1),
                jnp.concatenate([zeros, blocks[1]], axis=1),
            ],
            axis=0,
        )
        near = jnp.dot(v[c, hh], weighted, preferred_element_type=F32)
        near_ref[c, pl.ds(head * 128, 128), :] = near


def project_kernel(count, relatives, seq, pick, heads_step, heads):
    chunks = len(relatives)

    def body(*refs):
        xs = refs[:count]
        w_ref, wt_ref = refs[count : count + 2]
        q_ref, near_ref, state_ref, wt_out, held, scales = refs[count + 2 :]
        step = pl.program_id(0)

        @pl.when(step == 0)
        def _():
            at = 0
            for x_ref in xs:
                held[pl.ds(at, x_ref.shape[1]), :] = x_ref[pick]
                at += x_ref.shape[1]
            row_scales(xs, pick, scales)

        x = held[...]
        queries = jnp.dot(
            x, columns(w_ref, step * (heads_step * 128), heads_step * 128), preferred_element_type=F32
        )
        kv = jnp.dot(
            x,
            columns(w_ref, heads * 128 + step * (heads_step * 256), heads_step * 256),
            preferred_element_type=F32,
        )
        q, k, v = {}, {}, {}
        for c in range(chunks):
            scale = scales[c, 0:1, :]
            heads_now = pl.ds(step * heads_step, heads_step)
            wt_out[c, heads_now] = wt_ref[seq, place_of(relatives[c]), heads_now] * scale
            rows = slice(c * ROWS, (c + 1) * ROWS)
            for hh in range(heads_step):
                head = step * heads_step + hh
                q[c, hh] = queries[rows, hh * 128 : (hh + 1) * 128].T.astype(BF16)
                k[c, hh], v[c, hh] = split_keys(kv, scale, rows, hh)
                q_ref[c, pl.ds(head * 128, 128), :] = q[c, hh]
        for c, hh in q:
            state_ref[c, step * heads_step + hh] = jnp.dot(
                v[c, hh], k[c, hh], preferred_element_type=F32
            )
        near_parts(q, k, v, wt_out, near_ref, step, heads_step)

    return body


def keys_kernel(count, relative, seq, heads):
    def body(*refs):
        xs = refs[:count]
        w_ref, wt_ref = refs[count : count + 2]
        state_ref, k_ref, v_ref, wt_out, held, scales = refs[count + 2 :]
        at = 0
        for x_ref in xs:
            held[pl.ds(at, x_ref.shape[1]), :] = x_ref[0]
            at += x_ref.shape[1]
        kv = jnp.dot(
            held[...], w_ref[:, heads * 128 : heads * 384], preferred_element_type=F32
        )
        row_scales(xs, 0, scales)
        scale = scales[0, 0:1, :]
        wt_out[0] = wt_ref[seq, place_of(relative)] * scale
        for head in range(heads):
            k, v = split_keys(kv, scale, slice(0, ROWS), head)
            k_ref[head] = k
            v_ref[head] = v
            state_ref[0, head] = jnp.dot(v, k, preferred_element_type=F32)

    return body


def queries_kernel(heads_step):
    def body(held, w_ref, k_ref, v_ref, wt_out, q_ref, near_ref):
        step = pl.program_id(0)
        queries = jnp.dot(
            held[...],
            columns(w_ref, step * (heads_step * 128), heads_step * 128),
            preferred_element_type=F32,
        )
        q, k, v = {}, {}, {}
        for hh in range(heads_step):
            head = step * heads_step + hh
            q[0, hh] = queries[:, hh * 128 : (hh + 1) * 128].T.astype(BF16)
            q_ref[0, pl.ds(head * 128, 128), :] = q[0, hh]
            k[0, hh], v[0, hh] = k_ref[head], v_ref[head]
        near_parts(q, k, v, wt_out, near_ref, step, heads_step)

    return body


def vmem_call(body, steps, args, outs, scratch=(), limit=16):
    return pl.pallas_call(
        body,
        grid=(steps,),
        in_specs=[pl.BlockSpec(memory_space=pltpu.VMEM)] * len(args),
        out_specs=[pl.BlockSpec(memory_space=pltpu.VMEM)] * len(outs),
        out_shape=[pltpu.VMEM(shape, dtype) for shape, dtype in outs],
        scratch_shapes=list(scratch),
        compiler_params=pltpu.CompilerParams(vmem_limit_bytes=limit << 20),
    )(*args)


def project(xs, seq, relatives, weight, wt, pick=0, states_first=False):
    chunks = len(relatives)
    width, cols = weight.shape
    heads = cols // 384
    heads_step = 2 if heads % 2 == 0 else 1
    steps = heads // heads_step
    weight = in_vmem(weight)
    levels = (chunks, heads, wt.shape[3], ROWS)
    queries, states = (chunks, heads * 128, ROWS), (chunks, heads, 128, 128)
    held, scales = ((chunks * ROWS, width), BF16), pltpu.VMEM((chunks, 8, ROWS), F32)
    if states_first:
        state, k, v, scaled, held = vmem_call(
            keys_kernel(len(xs), relatives[0], seq, heads),
            1,
            [*xs, weight, wt],
            [
                (states, F32),
                ((heads, ROWS, 128), BF16),
                ((heads, 128, ROWS), BF16),
                (levels, F32),
                held,
            ],
            [scales],
        )
        q, near = vmem_call(
            queries_kernel(heads_step),
            steps,
            [in_vmem(held), weight, in_vmem(k), in_vmem(v), in_vmem(scaled)],
            [(queries, BF16), (queries, F32)],
        )
        return q, near, state, scaled
    return vmem_call(
        project_kernel(len(xs), relatives, seq, pick, heads_step, heads),
        steps,
        [*xs, weight, wt],
        [(queries, BF16), (queries, F32), (states, F32), (levels, F32)],
        [pltpu.VMEM(*held), scales],
    )


BEFORE = (1, 3, 0, 2)


def scaled_levels(q, wt_ref, c, head, levels):
    q16 = q.reshape(8, 16, ROWS)
    scaled = []
    for level in levels:
        row = jnp.broadcast_to(wt_ref[c, head, level : level + 1, :], (16, ROWS)).astype(BF16)
        scaled.append((q16 * row[None]).reshape(128, ROWS))
    return jnp.concatenate(scaled, axis=0)


def part_kernel(picks, half_heads):
    def body(*refs):
        qs, nears, states, wts = refs[0:4], refs[4:8], refs[8:12], refs[12:16]
        core_ref, mine_ref, other_ref = refs[16:19]
        out_ref = refs[-1]
        head = pl.program_id(0)
        rows = pl.ds(head * 128, 128)
        core = lax.axis_index("seq") % 2
        places = [place_of(r) for r in range(4)]
        st = [states[r][picks[r], head] for r in range(4)]
        buckets = [(core_ref[head].astype(F32) * core.astype(F32)).astype(BF16)]
        for j in range(mine_ref.shape[0]):
            at = head % half_heads
            buckets.append(jnp.where(head // half_heads == core, mine_ref[j, at], other_ref[j, at]))
        for r in range(4):
            place = places[r]
            level9 = st[BEFORE[r]] * (place % 2).astype(F32)
            upper = (place // 2).astype(F32)
            level10 = sum(
                [st[o] * (upper * (1 - places[o] // 2).astype(F32)) for o in range(4) if o != r]
            )
            mats = jnp.concatenate([level9.astype(BF16), level10.astype(BF16)] + buckets, axis=1)
            scaled = scaled_levels(
                qs[r][picks[r], rows, :], wts[r], picks[r], head, range(9, 11 + len(buckets))
            )
            out_ref[r, rows, :] = nears[r][picks[r], rows, :] + jnp.dot(
                mats, scaled, preferred_element_type=F32
            )

    return body


def last_kernel(picks, half_heads, seq, first_level, mine):
    def body(lengths_ref, *refs):
        qs, wts = refs[0:4], refs[4:8]
        part_ref, level_ref = refs[8:10]
        out_ref, buf, sem = refs[-3:]
        core = lax.axis_index("seq") % 2
        half = core if mine else 1 - core
        limit = lengths_ref[seq] - lax.axis_index("seq") * (4 * ROWS)
        levels = range(first_level, first_level + level_ref.shape[0])
        lane = lax.broadcasted_iota(jnp.int32, (1, ROWS), 1)
        copies = []
        for j in range(half_heads):
            head = half * half_heads + j
            rows = pl.ds(pl.multiple_of(head * 128, 128), 128)
            mats = jnp.concatenate([level_ref[i, j] for i in range(len(levels))], axis=1)
            for r in range(4):
                place = place_of(r)
                scaled = scaled_levels(
                    qs[r][picks[r], rows, :], wts[r], picks[r], head, levels
                )
                acc = part_ref[r, rows, :] + jnp.dot(mats, scaled, preferred_element_type=F32)
                scale = lax.rsqrt(jnp.mean(acc * acc, 0, keepdims=True) + 1e-06)
                valid = place * ROWS + lane < limit
                acc = acc * jnp.where(valid, scale, 0.0)
                buf[j, place] = acc.astype(BF16).T
            copies.append(
                pltpu.make_async_copy(buf.at[j], out_ref.at[seq, :, :, rows], sem.at[j])
            )
            copies[-1].start()
        for copy in copies:
            copy.wait()

    return body


def far(lengths, chunks, found, seq, out_prev, seqs):
    core_bucket, x_levels, x_other, y_levels, y_other = found
    heads = core_bucket.shape[0]
    half_heads = heads // 2
    picks = [c for _, c in chunks]
    vmem = pl.BlockSpec(memory_space=pltpu.VMEM)
    columns = [[in_vmem(call[i]) for call, _ in chunks] for i in range(4)]
    args = columns[0] + columns[1] + columns[2] + columns[3] + [core_bucket, x_levels, x_other]
    part = pl.pallas_call(
        part_kernel(picks, half_heads),
        grid=(heads,),
        in_specs=[vmem] * len(args),
        out_specs=vmem,
        out_shape=pltpu.VMEM((4, heads * 128, ROWS), F32),
        compiler_params=pltpu.CompilerParams(vmem_limit_bytes=4 << 20),
        name="far_part",
    )(*args)
    out = out_prev
    for mine, levels in ((True, y_levels), (False, y_other)):
        args = [lengths] + columns[0] + columns[3] + [in_vmem(part), in_vmem(levels)]
        in_specs = [pl.BlockSpec(memory_space=pltpu.SMEM)] + [vmem] * (len(args) - 1)
        aliases = {}
        if out is not None:
            in_specs.append(pl.BlockSpec(memory_space=pl.ANY))
            args.append(out)
            aliases = {len(args) - 1: 0}
        out = pl.pallas_call(
            last_kernel(picks, half_heads, seq, 12 + x_levels.shape[0], mine),
            in_specs=in_specs,
            out_specs=pl.BlockSpec(memory_space=pl.ANY),
            out_shape=jax.ShapeDtypeStruct((seqs, 4, ROWS, heads * 128), BF16),
            scratch_shapes=[
                pltpu.VMEM((half_heads, 4, ROWS, 128), BF16),
                pltpu.SemaphoreType.DMA((half_heads,)),
            ],
            input_output_aliases=aliases,
            compiler_params=pltpu.CompilerParams(vmem_limit_bytes=6 << 20),
            name="far_last",
        )(*args)
    return out


def small_call(body, outs, *args):
    return vmem_call(body, 1, [in_vmem(x) for x in args], outs, limit=4)


def seq_bit(j):
    return (lax.axis_index("seq") // (1 << j)) % 2


def total_kernel(own_ref, ab_ref, cd_ref, total_ref, sent_ref):
    total = own_ref[0] + ab_ref[0] + ab_ref[1] + cd_ref[0]
    total_ref[...] = total
    sent_ref[...] = total.astype(BF16)


def core_kernel(total_ref, received_ref, part_ref, sent_ref):
    half = part_ref.shape[0]
    heads = pl.ds(seq_bit(0) * half, half)
    part = total_ref[heads] + received_ref[heads].astype(F32)
    part_ref[...] = part
    sent_ref[...] = part.astype(BF16)


def stage_kernel(low, last):
    def body(part_ref, one_ref, two_ref, three_ref, mine_ref, *outs):
        one, two, three = [r[...].astype(F32) for r in (one_ref, two_ref, three_ref)]
        mine_ref[0] = (one * seq_bit(low).astype(F32)).astype(BF16)
        mine_ref[1] = ((two + three) * seq_bit(low + 1).astype(F32)).astype(BF16)
        if not last:
            next_ref, sent_ref = outs
            part = part_ref[...] + (one + (two + three))
            next_ref[...] = part
            sent_ref[...] = part.astype(BF16)

    return body


def exchange(own, ab, cd):
    size = lax.axis_size("seq")
    heads = own.shape[1]
    whole, half = (heads, 128, 128), (heads // 2, 128, 128)

    def swap(value, mask):
        return lax.ppermute(value, "seq", [(i, i ^ mask) for i in range(size)])

    total, sent = small_call(total_kernel, [(whole, F32), (whole, BF16)], own, ab, cd)
    core_bucket = swap(sent, 1)
    part, sent = small_call(core_kernel, [(half, F32), (half, BF16)], total, core_bucket)
    found = [core_bucket]
    for low in (1, 3):
        heard = [swap(sent, mask << low) for mask in (1, 2, 3)]
        outs = [((2,) + half, BF16), (half, F32), (half, BF16)]
        made = small_call(stage_kernel(low, low == 3), outs[: 1 if low == 3 else 3], part, *heard)
        found += [made[0], swap(made[0], 1)]
        if low == 1:
            part, sent = made[1:]
    return found


def on_device(tokens, norm_gain, projection, level_table, level_index, lengths):
    seqs, row_count, _ = tokens.shape
    tables, heads, level_total = level_table.shape
    groups = lax.axis_size("head")
    half = row_count // 2
    up = [(i, (i + 1) % groups) for i in range(groups)]
    down = [(i, (i - 1) % groups) for i in range(groups)]

    got = []
    held = tokens
    for s in range(seqs):
        low, high = held[s : s + 1, :half], held[s : s + 1, half:]
        a_low = lax.ppermute(low, "head", up)
        b_high = lax.ppermute(high, "head", down)
        a_high = lax.ppermute(high, "head", up)
        b_low = lax.ppermute(low, "head", down)
        if s + 1 < seqs:
            held, a_low, b_high = lax.optimization_barrier((tokens, a_low, b_high))
        c = lax.ppermute(a_low, "head", up)
        d = lax.ppermute(b_high, "head", down)
        got.append(([a_low, a_high, b_low, b_high], [c, d]))

    level_rows = -(-level_total // 8) * 8
    onehot = (level_index[..., None] == jnp.arange(tables, dtype=jnp.int32)).astype(F32)
    table = jnp.pad(level_table, ((0, 0), (0, 0), (0, level_rows - level_total)))
    wt = jnp.einsum(
        "ghl,szrg->szhlr",
        table,
        onehot.reshape(seqs, groups, row_count, tables),
        precision=lax.Precision.HIGHEST,
    )

    weight = fold_gain(norm_gain, projection)

    own = []
    for s in range(seqs):
        own.append(project([tokens], s, [0], weight, wt, s))
    parts = []
    for s in range(seqs):
        ab = project(got[s][0], s, [1, 2], weight, wt)
        cd = project(got[s][1], s, [3], weight, wt, states_first=s + 1 == seqs)
        parts.append((ab, cd))

    out = None
    for s in range(seqs):
        ab, cd = parts[s]
        found = exchange(own[s][2], ab[2], cd[2])
        chunks = [(own[s], 0), (ab, 0), (ab, 1), (cd, 0)]
        out = far(lengths, chunks, found, s, out, seqs)
    return out.reshape(seqs, row_count * groups, heads * 128)


def solution(mesh):
    in_specs = (
        P(None, ("seq", "head"), None),
        P(),
        P(None, "head"),
        P(None, "head", None),
        P(None, "seq"),
        P(),
    )
    out_specs = P(None, "seq", "head")

    return jax.shard_map(on_device, mesh=mesh, in_specs=in_specs, out_specs=out_specs, check_vma=False)
```

```python
import jax
import jax.numpy as jnp
from jax import lax
from jax.experimental import pallas as pl
from jax.experimental.pallas import tpu as pltpu
from jax.sharding import PartitionSpec as P


TILE = 128
ROWS = 2 * TILE
F32 = jnp.float32
BF16 = jnp.bfloat16
NT = (((1,), (1,)), ((), ()))


def in_vmem(value):
    return pltpu.with_memory_space_constraint(value, pltpu.VMEM)


def fold_kernel(gain_ref, w_ref, out_ref):
    heads = w_ref.shape[1] // (3 * TILE)
    for at in range(0, w_ref.shape[0], TILE):
        column = jnp.broadcast_to(gain_ref[:, at : at + TILE], (TILE, TILE)).T
        for lane in range(0, w_ref.shape[1], TILE):
            part = w_ref[at : at + TILE, lane : lane + TILE].astype(F32) * column
            head, which = divmod(lane // TILE, 3)
            to = head * TILE if which == 0 else heads * TILE + head * 2 * TILE + (which - 1) * TILE
            out_ref[at : at + TILE, to : to + TILE] = part.astype(BF16)


def fold_gain(gain, projection):
    width, cols = projection.shape
    return pl.pallas_call(
        fold_kernel,
        grid=(width // ROWS,),
        in_specs=[
            pl.BlockSpec((1, ROWS), lambda i: (0, i)),
            pl.BlockSpec((ROWS, cols), lambda i: (i, 0)),
        ],
        out_specs=pl.BlockSpec((ROWS, cols), lambda i: (i, 0)),
        out_shape=pltpu.VMEM((width, cols), BF16),
        compiler_params=pltpu.CompilerParams(vmem_limit_bytes=8 << 20),
        name="fold_gain",
    )(gain.reshape(1, width), pltpu.with_memory_space_constraint(projection, pltpu.HBM))


def place_of(relative):
    return (lax.axis_index("head") + (0, 3, 1, 2)[relative]) % 4


def row_scales(xs, pick, scales):
    sums = []
    for x_ref in xs:
        total = jnp.zeros((x_ref.shape[1], TILE), F32)
        for lane in range(0, x_ref.shape[2], TILE):
            part = x_ref[pick, :, lane : lane + TILE].astype(F32)
            total = total + part * part
        sums.append(total)
    sums = jnp.concatenate(sums, axis=0)
    ones = jnp.full((8, TILE), 1.0, F32)
    for c in range(scales.shape[0]):
        mean = lax.dot_general(
            ones,
            sums[c * ROWS : (c + 1) * ROWS],
            NT,
            precision=lax.Precision.HIGHEST,
            preferred_element_type=F32,
        ) * (1.0 / xs[0].shape[2])
        scales[c] = lax.rsqrt(mean + 1e-06)


def columns(w_ref, start, count):
    return w_ref[:, pl.ds(pl.multiple_of(start, TILE), count)]


def split_keys(kv, scale, rows, hh):
    at = hh * 256
    k = kv[rows, at : at + 128].astype(BF16)
    v = (kv[rows, at + 128 : at + 256].T * (scale * scale)).astype(BF16)
    return k, v


def near_parts(q, k, v, wt_out, near_ref, step, heads_step):
    source = lax.broadcasted_iota(jnp.int32, (TILE, TILE), 0)
    target = lax.broadcasted_iota(jnp.int32, (TILE, TILE), 1)
    differ = jnp.bitwise_xor(source, target)
    causal = source <= target
    zeros = jnp.zeros((TILE, TILE), BF16)
    scores = {i: jnp.dot(k[i], q[i], preferred_element_type=F32) for i in q}
    for c, hh in q:
        head = step * heads_step + hh
        blocks = []
        for t in range(2):
            lanes = slice(t * TILE, (t + 1) * TILE)
            grid = wt_out[c, head, 0:1, lanes]
            for level in range(1, 8):
                row = wt_out[c, head, level : level + 1, lanes]
                grid = jnp.where(differ >= 1 << (level - 1), row, grid)
            grid = jnp.where(causal, grid, 0.0)
            blocks.append((scores[c, hh][lanes, lanes] * grid).astype(BF16))
        row = wt_out[c, head, 8:9, TILE:]
        cross = (scores[c, hh][:TILE, TILE:] * row).astype(BF16)
        weighted = jnp.concatenate(
            [
                jnp.concatenate([blocks[0], cross], axis=1),
                jnp.concatenate([zeros, blocks[1]], axis=1),
            ],
            axis=0,
        )
        near = jnp.dot(v[c, hh], weighted, preferred_element_type=F32)
        near_ref[c, pl.ds(head * 128, 128), :] = near


def project_kernel(count, relatives, seq, pick, heads_step, heads):
    chunks = len(relatives)

    def body(*refs):
        xs = refs[:count]
        w_ref, wt_ref = refs[count : count + 2]
        q_ref, near_ref, state_ref, wt_out, held, scales = refs[count + 2 :]
        step = pl.program_id(0)

        @pl.when(step == 0)
        def _():
            at = 0
            for x_ref in xs:
                held[pl.ds(at, x_ref.shape[1]), :] = x_ref[pick]
                at += x_ref.shape[1]
            row_scales(xs, pick, scales)

        x = held[...]
        queries = jnp.dot(
            x, columns(w_ref, step * (heads_step * 128), heads_step * 128), preferred_element_type=F32
        )
        kv = jnp.dot(
            x,
            columns(w_ref, heads * 128 + step * (heads_step * 256), heads_step * 256),
            preferred_element_type=F32,
        )
        q, k, v = {}, {}, {}
        for c in range(chunks):
            scale = scales[c, 0:1, :]
            heads_now = pl.ds(step * heads_step, heads_step)
            wt_out[c, heads_now] = wt_ref[seq, place_of(relatives[c]), heads_now] * scale
            rows = slice(c * ROWS, (c + 1) * ROWS)
            for hh in range(heads_step):
                head = step * heads_step + hh
                q[c, hh] = queries[rows, hh * 128 : (hh + 1) * 128].T.astype(BF16)
                k[c, hh], v[c, hh] = split_keys(kv, scale, rows, hh)
                q_ref[c, pl.ds(head * 128, 128), :] = q[c, hh]
        for c, hh in q:
            state_ref[c, step * heads_step + hh] = jnp.dot(
                v[c, hh], k[c, hh], preferred_element_type=F32
            )
        near_parts(q, k, v, wt_out, near_ref, step, heads_step)

    return body


def keys_kernel(count, relative, seq, heads):
    def body(*refs):
        xs = refs[:count]
        w_ref, wt_ref = refs[count : count + 2]
        state_ref, k_ref, v_ref, wt_out, held, scales = refs[count + 2 :]
        at = 0
        for x_ref in xs:
            held[pl.ds(at, x_ref.shape[1]), :] = x_ref[0]
            at += x_ref.shape[1]
        kv = jnp.dot(
            held[...], w_ref[:, heads * 128 : heads * 384], preferred_element_type=F32
        )
        row_scales(xs, 0, scales)
        scale = scales[0, 0:1, :]
        wt_out[0] = wt_ref[seq, place_of(relative)] * scale
        for head in range(heads):
            k, v = split_keys(kv, scale, slice(0, ROWS), head)
            k_ref[head] = k
            v_ref[head] = v
            state_ref[0, head] = jnp.dot(v, k, preferred_element_type=F32)

    return body


def queries_kernel(heads_step):
    def body(held, w_ref, k_ref, v_ref, wt_out, q_ref, near_ref):
        step = pl.program_id(0)
        queries = jnp.dot(
            held[...],
            columns(w_ref, step * (heads_step * 128), heads_step * 128),
            preferred_element_type=F32,
        )
        q, k, v = {}, {}, {}
        for hh in range(heads_step):
            head = step * heads_step + hh
            q[0, hh] = queries[:, hh * 128 : (hh + 1) * 128].T.astype(BF16)
            q_ref[0, pl.ds(head * 128, 128), :] = q[0, hh]
            k[0, hh], v[0, hh] = k_ref[head], v_ref[head]
        near_parts(q, k, v, wt_out, near_ref, step, heads_step)

    return body


def vmem_call(body, steps, args, outs, scratch=(), limit=16):
    return pl.pallas_call(
        body,
        grid=(steps,),
        in_specs=[pl.BlockSpec(memory_space=pltpu.VMEM)] * len(args),
        out_specs=[pl.BlockSpec(memory_space=pltpu.VMEM)] * len(outs),
        out_shape=[pltpu.VMEM(shape, dtype) for shape, dtype in outs],
        scratch_shapes=list(scratch),
        compiler_params=pltpu.CompilerParams(vmem_limit_bytes=limit << 20),
    )(*args)


def project(xs, seq, relatives, weight, wt, pick=0, states_first=False):
    chunks = len(relatives)
    width, cols = weight.shape
    heads = cols // 384
    heads_step = 2 if heads % 2 == 0 else 1
    steps = heads // heads_step
    weight = in_vmem(weight)
    levels = (chunks, heads, wt.shape[3], ROWS)
    queries, states = (chunks, heads * 128, ROWS), (chunks, heads, 128, 128)
    held, scales = ((chunks * ROWS, width), BF16), pltpu.VMEM((chunks, 8, ROWS), F32)
    if states_first:
        state, k, v, scaled, held = vmem_call(
            keys_kernel(len(xs), relatives[0], seq, heads),
            1,
            [*xs, weight, wt],
            [
                (states, F32),
                ((heads, ROWS, 128), BF16),
                ((heads, 128, ROWS), BF16),
                (levels, F32),
                held,
            ],
            [scales],
        )
        q, near = vmem_call(
            queries_kernel(heads_step),
            steps,
            [in_vmem(held), weight, in_vmem(k), in_vmem(v), in_vmem(scaled)],
            [(queries, BF16), (queries, F32)],
        )
        return q, near, state, scaled
    return vmem_call(
        project_kernel(len(xs), relatives, seq, pick, heads_step, heads),
        steps,
        [*xs, weight, wt],
        [(queries, BF16), (queries, F32), (states, F32), (levels, F32)],
        [pltpu.VMEM(*held), scales],
    )


BEFORE = (1, 3, 0, 2)


def scaled_levels(q, wt_ref, c, head, levels):
    q16 = q.reshape(8, 16, ROWS)
    scaled = []
    for level in levels:
        row = jnp.broadcast_to(wt_ref[c, head, level : level + 1, :], (16, ROWS)).astype(BF16)
        scaled.append((q16 * row[None]).reshape(128, ROWS))
    return jnp.concatenate(scaled, axis=0)


def part_kernel(picks, half_heads):
    def body(*refs):
        qs, nears, states, wts = refs[0:4], refs[4:8], refs[8:12], refs[12:16]
        core_ref, mine_ref, other_ref = refs[16:19]
        out_ref = refs[-1]
        head = pl.program_id(0)
        rows = pl.ds(head * 128, 128)
        core = lax.axis_index("seq") % 2
        places = [place_of(r) for r in range(4)]
        st = [states[r][picks[r], head] for r in range(4)]
        buckets = [(core_ref[head].astype(F32) * core.astype(F32)).astype(BF16)]
        for j in range(mine_ref.shape[0]):
            at = head % half_heads
            buckets.append(jnp.where(head // half_heads == core, mine_ref[j, at], other_ref[j, at]))
        for r in range(4):
            place = places[r]
            level9 = st[BEFORE[r]] * (place % 2).astype(F32)
            upper = (place // 2).astype(F32)
            level10 = sum(
                [st[o] * (upper * (1 - places[o] // 2).astype(F32)) for o in range(4) if o != r]
            )
            mats = jnp.concatenate([level9.astype(BF16), level10.astype(BF16)] + buckets, axis=1)
            scaled = scaled_levels(
                qs[r][picks[r], rows, :], wts[r], picks[r], head, range(9, 11 + len(buckets))
            )
            out_ref[r, rows, :] = nears[r][picks[r], rows, :] + jnp.dot(
                mats, scaled, preferred_element_type=F32
            )

    return body


def finish_half(lengths_ref, refs, picks, half_heads, seq, first_level, half, done):
    qs, wts = refs[0:4], refs[4:8]
    part_ref, level_ref = refs[8:10]
    limit = lengths_ref[seq] - lax.axis_index("seq") * (4 * ROWS)
    levels = range(first_level, first_level + level_ref.shape[0])
    lane = lax.broadcasted_iota(jnp.int32, (1, ROWS), 1)
    for j in range(half_heads):
        head = half * half_heads + j
        rows = pl.ds(pl.multiple_of(head * 128, 128), 128)
        mats = jnp.concatenate([level_ref[i, j] for i in range(len(levels))], axis=1)
        for r in range(4):
            place = place_of(r)
            scaled = scaled_levels(qs[r][picks[r], rows, :], wts[r], picks[r], head, levels)
            acc = part_ref[r, rows, :] + jnp.dot(mats, scaled, preferred_element_type=F32)
            scale = lax.rsqrt(jnp.mean(acc * acc, 0, keepdims=True) + 1e-06)
            valid = place * ROWS + lane < limit
            acc = acc * jnp.where(valid, scale, 0.0)
            done(j, r, place, acc.astype(BF16).T)


def mine_kernel(picks, half_heads, seq, first_level):
    def body(lengths_ref, *refs):
        out_ref = refs[-1]

        def done(j, r, place, rows):
            out_ref[j, place] = rows

        core = lax.axis_index("seq") % 2
        finish_half(lengths_ref, refs, picks, half_heads, seq, first_level, core, done)

    return body


def last_kernel(picks, half_heads, seq, first_level):
    def body(lengths_ref, *refs):
        mine_ref = refs[10]
        out_ref, buf, sem, mine_sem = refs[-4:]
        core = lax.axis_index("seq") % 2
        copies = []

        def lanes(half, j):
            return pl.ds(pl.multiple_of((half * half_heads + j) * 128, 128), 128)

        for j in range(half_heads):
            copies.append(
                pltpu.make_async_copy(
                    mine_ref.at[j], out_ref.at[seq, :, :, lanes(core, j)], mine_sem.at[j]
                )
            )
            copies[-1].start()

        def done(j, r, place, rows):
            buf[j, r] = rows
            copies.append(
                pltpu.make_async_copy(
                    buf.at[j, r], out_ref.at[seq, place, :, lanes(1 - core, j)], sem.at[j, r]
                )
            )
            copies[-1].start()

        finish_half(lengths_ref, refs, picks, half_heads, seq, first_level, 1 - core, done)
        for copy in copies:
            copy.wait()

    return body


def far(lengths, chunks, found, seq, out_prev, seqs):
    core_bucket, x_levels, x_other, y_levels, y_other = found
    heads = core_bucket.shape[0]
    half_heads = heads // 2
    picks = [c for _, c in chunks]
    vmem = pl.BlockSpec(memory_space=pltpu.VMEM)
    columns = [[in_vmem(call[i]) for call, _ in chunks] for i in range(4)]
    args = columns[0] + columns[1] + columns[2] + columns[3] + [core_bucket, x_levels, x_other]
    part = pl.pallas_call(
        part_kernel(picks, half_heads),
        grid=(heads,),
        in_specs=[vmem] * len(args),
        out_specs=vmem,
        out_shape=pltpu.VMEM((4, heads * 128, ROWS), F32),
        compiler_params=pltpu.CompilerParams(vmem_limit_bytes=4 << 20),
        name="far_part",
    )(*args)
    first_level = 12 + x_levels.shape[0]
    smem = pl.BlockSpec(memory_space=pltpu.SMEM)
    half_shape = (half_heads, 4, ROWS, 128)
    args = [lengths] + columns[0] + columns[3] + [in_vmem(part), in_vmem(y_levels)]
    mine = pl.pallas_call(
        mine_kernel(picks, half_heads, seq, first_level),
        in_specs=[smem] + [vmem] * (len(args) - 1),
        out_specs=vmem,
        out_shape=pltpu.VMEM(half_shape, BF16),
        compiler_params=pltpu.CompilerParams(vmem_limit_bytes=4 << 20),
        name="far_mine",
    )(*args)
    args = args[:-1] + [in_vmem(y_other), in_vmem(mine)]
    in_specs = [smem] + [vmem] * (len(args) - 1)
    aliases = {}
    if out_prev is not None:
        in_specs.append(pl.BlockSpec(memory_space=pl.ANY))
        args.append(out_prev)
        aliases = {len(args) - 1: 0}
    return pl.pallas_call(
        last_kernel(picks, half_heads, seq, first_level),
        in_specs=in_specs,
        out_specs=pl.BlockSpec(memory_space=pl.ANY),
        out_shape=jax.ShapeDtypeStruct((seqs, 4, ROWS, heads * 128), BF16),
        scratch_shapes=[
            pltpu.VMEM(half_shape, BF16),
            pltpu.SemaphoreType.DMA((half_heads, 4)),
            pltpu.SemaphoreType.DMA((half_heads,)),
        ],
        input_output_aliases=aliases,
        compiler_params=pltpu.CompilerParams(vmem_limit_bytes=6 << 20),
        name="far_last",
    )(*args)


def small_call(body, outs, *args):
    return vmem_call(body, 1, [in_vmem(x) for x in args], outs, limit=4)


def seq_bit(j):
    return (lax.axis_index("seq") // (1 << j)) % 2


def total_kernel(own_ref, ab_ref, cd_ref, total_ref, sent_ref):
    total = own_ref[0] + ab_ref[0] + ab_ref[1] + cd_ref[0]
    total_ref[...] = total
    sent_ref[...] = total.astype(BF16)


def core_kernel(total_ref, received_ref, part_ref, sent_ref):
    half = part_ref.shape[0]
    heads = pl.ds(seq_bit(0) * half, half)
    part = total_ref[heads] + received_ref[heads].astype(F32)
    part_ref[...] = part
    sent_ref[...] = part.astype(BF16)


def stage_kernel(low, last):
    def body(part_ref, one_ref, two_ref, three_ref, mine_ref, *outs):
        one, two, three = [r[...].astype(F32) for r in (one_ref, two_ref, three_ref)]
        mine_ref[0] = (one * seq_bit(low).astype(F32)).astype(BF16)
        mine_ref[1] = ((two + three) * seq_bit(low + 1).astype(F32)).astype(BF16)
        if not last:
            next_ref, sent_ref = outs
            part = part_ref[...] + (one + (two + three))
            next_ref[...] = part
            sent_ref[...] = part.astype(BF16)

    return body


def exchange(own, ab, cd):
    size = lax.axis_size("seq")
    heads = own.shape[1]
    whole, half = (heads, 128, 128), (heads // 2, 128, 128)

    def swap(value, mask):
        return lax.ppermute(value, "seq", [(i, i ^ mask) for i in range(size)])

    total, sent = small_call(total_kernel, [(whole, F32), (whole, BF16)], own, ab, cd)
    core_bucket = swap(sent, 1)
    part, sent = small_call(core_kernel, [(half, F32), (half, BF16)], total, core_bucket)
    found = [core_bucket]
    for low in (1, 3):
        heard = [swap(sent, mask << low) for mask in (1, 2, 3)]
        outs = [((2,) + half, BF16), (half, F32), (half, BF16)]
        made = small_call(stage_kernel(low, low == 3), outs[: 1 if low == 3 else 3], part, *heard)
        found += [made[0], swap(made[0], 1)]
        if low == 1:
            part, sent = made[1:]
    return found


def on_device(tokens, norm_gain, projection, level_table, level_index, lengths):
    seqs, row_count, _ = tokens.shape
    tables, heads, level_total = level_table.shape
    groups = lax.axis_size("head")
    half = row_count // 2
    up = [(i, (i + 1) % groups) for i in range(groups)]
    down = [(i, (i - 1) % groups) for i in range(groups)]

    got = []
    held = tokens
    for s in range(seqs):
        low, high = held[s : s + 1, :half], held[s : s + 1, half:]
        a_low = lax.ppermute(low, "head", up)
        b_high = lax.ppermute(high, "head", down)
        a_high = lax.ppermute(high, "head", up)
        b_low = lax.ppermute(low, "head", down)
        if s + 1 < seqs:
            held, a_low, b_high = lax.optimization_barrier((tokens, a_low, b_high))
        c = lax.ppermute(a_low, "head", up)
        d = lax.ppermute(b_high, "head", down)
        got.append(([a_low, a_high, b_low, b_high], [c, d]))

    level_rows = -(-level_total // 8) * 8
    onehot = (level_index[..., None] == jnp.arange(tables, dtype=jnp.int32)).astype(F32)
    table = jnp.pad(level_table, ((0, 0), (0, 0), (0, level_rows - level_total)))
    wt = jnp.einsum(
        "ghl,szrg->szhlr",
        table,
        onehot.reshape(seqs, groups, row_count, tables),
        precision=lax.Precision.HIGHEST,
    )

    weight = fold_gain(norm_gain, projection)

    own = []
    for s in range(seqs):
        own.append(project([tokens], s, [0], weight, wt, s))
    parts = []
    for s in range(seqs):
        ab = project(got[s][0], s, [1, 2], weight, wt)
        cd = project(got[s][1], s, [3], weight, wt, states_first=s + 1 == seqs)
        parts.append((ab, cd))

    out = None
    for s in range(seqs):
        ab, cd = parts[s]
        found = exchange(own[s][2], ab[2], cd[2])
        chunks = [(own[s], 0), (ab, 0), (ab, 1), (cd, 0)]
        out = far(lengths, chunks, found, s, out, seqs)
    return out.reshape(seqs, row_count * groups, heads * 128)


def solution(mesh):
    in_specs = (
        P(None, ("seq", "head"), None),
        P(),
        P(None, "head"),
        P(None, "head", None),
        P(None, "seq"),
        P(),
    )
    out_specs = P(None, "seq", "head")

    return jax.shard_map(on_device, mesh=mesh, in_specs=in_specs, out_specs=out_specs, check_vma=False)
```

```python
import jax
import jax.numpy as jnp
from jax import lax
from jax.experimental import pallas as pl
from jax.experimental.pallas import tpu as pltpu
from jax.sharding import PartitionSpec as P


TILE = 128
ROWS = 2 * TILE
F32 = jnp.float32
BF16 = jnp.bfloat16
NT = (((1,), (1,)), ((), ()))


def in_vmem(value):
    return pltpu.with_memory_space_constraint(value, pltpu.VMEM)


def fold_kernel(gain_ref, w_ref, out_ref):
    heads = w_ref.shape[1] // (3 * TILE)
    for at in range(0, w_ref.shape[0], TILE):
        column = jnp.broadcast_to(gain_ref[:, at : at + TILE], (TILE, TILE)).T
        for lane in range(0, w_ref.shape[1], TILE):
            part = w_ref[at : at + TILE, lane : lane + TILE].astype(F32) * column
            head, which = divmod(lane // TILE, 3)
            to = head * TILE if which == 0 else heads * TILE + head * 2 * TILE + (which - 1) * TILE
            out_ref[at : at + TILE, to : to + TILE] = part.astype(BF16)


def fold_gain(gain, projection):
    width, cols = projection.shape
    return pl.pallas_call(
        fold_kernel,
        grid=(width // ROWS,),
        in_specs=[
            pl.BlockSpec((1, ROWS), lambda i: (0, i)),
            pl.BlockSpec((ROWS, cols), lambda i: (i, 0)),
        ],
        out_specs=pl.BlockSpec((ROWS, cols), lambda i: (i, 0)),
        out_shape=pltpu.VMEM((width, cols), BF16),
        compiler_params=pltpu.CompilerParams(vmem_limit_bytes=8 << 20),
        name="fold_gain",
    )(gain.reshape(1, width), pltpu.with_memory_space_constraint(projection, pltpu.HBM))


def place_of(relative):
    return (lax.axis_index("head") + (0, 3, 1, 2)[relative]) % 4


def row_scales(xs, blocks, scales):
    sums = []
    for piece, index, first, rows in blocks:
        total = jnp.zeros((rows, TILE), F32)
        for lane in range(0, xs[piece].shape[2], TILE):
            part = xs[piece][index, first : first + rows, lane : lane + TILE].astype(F32)
            total = total + part * part
        sums.append(total)
    sums = jnp.concatenate(sums, axis=0)
    ones = jnp.full((8, TILE), 1.0, F32)
    width = scales.shape[2]
    for c in range(scales.shape[0]):
        mean = lax.dot_general(
            ones,
            sums[c * width : (c + 1) * width],
            NT,
            precision=lax.Precision.HIGHEST,
            preferred_element_type=F32,
        ) * (1.0 / xs[0].shape[2])
        scales[c] = lax.rsqrt(mean + 1e-06)


def hold_rows(xs, blocks, held):
    at = 0
    for piece, index, first, rows in blocks:
        held[pl.ds(at, rows), :] = xs[piece][index, first : first + rows]
        at += rows


def columns(w_ref, start, count):
    return w_ref[:, pl.ds(pl.multiple_of(start, TILE), count)]


def split_keys(kv, scale, rows, hh):
    at = hh * 256
    k = kv[rows, at : at + 128].astype(BF16)
    v = (kv[rows, at + 128 : at + 256].T * (scale * scale)).astype(BF16)
    return k, v


def near_parts(q, k, v, wt_out, near_ref, step, heads_step):
    source = lax.broadcasted_iota(jnp.int32, (TILE, TILE), 0)
    target = lax.broadcasted_iota(jnp.int32, (TILE, TILE), 1)
    differ = jnp.bitwise_xor(source, target)
    causal = source <= target
    zeros = jnp.zeros((TILE, TILE), BF16)
    scores = {i: jnp.dot(k[i], q[i], preferred_element_type=F32) for i in q}
    for c, hh in q:
        head = step * heads_step + hh
        blocks = []
        for t in range(2):
            lanes = slice(t * TILE, (t + 1) * TILE)
            grid = wt_out[c, head, 0:1, lanes]
            for level in range(1, 8):
                row = wt_out[c, head, level : level + 1, lanes]
                grid = jnp.where(differ >= 1 << (level - 1), row, grid)
            grid = jnp.where(causal, grid, 0.0)
            blocks.append((scores[c, hh][lanes, lanes] * grid).astype(BF16))
        row = wt_out[c, head, 8:9, TILE:]
        cross = (scores[c, hh][:TILE, TILE:] * row).astype(BF16)
        weighted = jnp.concatenate(
            [
                jnp.concatenate([blocks[0], cross], axis=1),
                jnp.concatenate([zeros, blocks[1]], axis=1),
            ],
            axis=0,
        )
        near = jnp.dot(v[c, hh], weighted, preferred_element_type=F32)
        near_ref[c, pl.ds(head * 128, 128), :] = near


def project_kernel(count, relatives, seq, blocks, heads_step, heads):
    chunks = len(relatives)

    def body(*refs):
        xs = refs[:count]
        w_ref, wt_ref = refs[count : count + 2]
        q_ref, near_ref, state_ref, wt_out, held, scales = refs[count + 2 :]
        step = pl.program_id(0)

        @pl.when(step == 0)
        def _():
            hold_rows(xs, blocks, held)
            row_scales(xs, blocks, scales)

        x = held[...]
        queries = jnp.dot(
            x, columns(w_ref, step * (heads_step * 128), heads_step * 128), preferred_element_type=F32
        )
        kv = jnp.dot(
            x,
            columns(w_ref, heads * 128 + step * (heads_step * 256), heads_step * 256),
            preferred_element_type=F32,
        )
        q, k, v = {}, {}, {}
        for c in range(chunks):
            scale = scales[c, 0:1, :]
            heads_now = pl.ds(step * heads_step, heads_step)
            wt_out[c, heads_now] = wt_ref[seq, place_of(relatives[c]), heads_now] * scale
            rows = slice(c * ROWS, (c + 1) * ROWS)
            for hh in range(heads_step):
                head = step * heads_step + hh
                q[c, hh] = queries[rows, hh * 128 : (hh + 1) * 128].T.astype(BF16)
                k[c, hh], v[c, hh] = split_keys(kv, scale, rows, hh)
                q_ref[c, pl.ds(head * 128, 128), :] = q[c, hh]
        for c, hh in q:
            state_ref[c, step * heads_step + hh] = jnp.dot(
                v[c, hh], k[c, hh], preferred_element_type=F32
            )
        near_parts(q, k, v, wt_out, near_ref, step, heads_step)

    return body


def keys_kernel(relative, seq, tile, heads):
    lanes = slice(tile * TILE, (tile + 1) * TILE)

    def body(*refs):
        xs, (w_ref, wt_ref) = refs[:2], refs[2:4]
        before_ref = refs[4] if tile else None
        state_ref, k_ref, v_ref, wt_out, held, scales = refs[-6:]
        blocks = [(i, 0, 0, x_ref.shape[1]) for i, x_ref in enumerate(xs)]
        hold_rows(xs, blocks, held)
        kv = jnp.dot(
            held[...], w_ref[:, heads * 128 : heads * 384], preferred_element_type=F32
        )
        row_scales(xs, blocks, scales)
        scale = scales[0, 0:1, :]
        wt_out[...] = wt_ref[seq, place_of(relative), :, :, lanes] * scale
        for head in range(heads):
            k, v = split_keys(kv, scale, slice(0, TILE), head)
            k_ref[head] = k
            v_ref[head] = v
            state = jnp.dot(v, k, preferred_element_type=F32)
            state_ref[0, head] = state + before_ref[0, head] if tile else state

    return body


def queries_kernel(heads_step):
    def body(held_a, held_b, w_ref, k_a, k_b, v_a, v_b, wt_a, wt_b, q_ref, near_ref, wt_out, held):
        step = pl.program_id(0)

        @pl.when(step == 0)
        def _():
            held[0:TILE, :] = held_a[...]
            held[TILE:, :] = held_b[...]
            wt_out[0, :, :, 0:TILE] = wt_a[...]
            wt_out[0, :, :, TILE:] = wt_b[...]

        queries = jnp.dot(
            held[...],
            columns(w_ref, step * (heads_step * 128), heads_step * 128),
            preferred_element_type=F32,
        )
        q, k, v = {}, {}, {}
        for hh in range(heads_step):
            head = step * heads_step + hh
            q[0, hh] = queries[:, hh * 128 : (hh + 1) * 128].T.astype(BF16)
            q_ref[0, pl.ds(head * 128, 128), :] = q[0, hh]
            k[0, hh] = jnp.concatenate([k_a[head], k_b[head]], axis=0)
            v[0, hh] = jnp.concatenate([v_a[head], v_b[head]], axis=1)
        near_parts(q, k, v, wt_out, near_ref, step, heads_step)

    return body


def vmem_call(body, steps, args, outs, scratch=(), limit=16):
    return pl.pallas_call(
        body,
        grid=(steps,),
        in_specs=[pl.BlockSpec(memory_space=pltpu.VMEM)] * len(args),
        out_specs=[pl.BlockSpec(memory_space=pltpu.VMEM)] * len(outs),
        out_shape=[pltpu.VMEM(shape, dtype) for shape, dtype in outs],
        scratch_shapes=list(scratch),
        compiler_params=pltpu.CompilerParams(vmem_limit_bytes=limit << 20),
    )(*args)


def project(xs, seq, relatives, weight, wt, blocks):
    chunks = len(relatives)
    width, cols = weight.shape
    heads = cols // 384
    heads_step = 2 if heads % 2 == 0 else 1
    levels = (chunks, heads, wt.shape[3], ROWS)
    queries, states = (chunks, heads * 128, ROWS), (chunks, heads, 128, 128)
    return vmem_call(
        project_kernel(len(xs), relatives, seq, blocks, heads_step, heads),
        heads // heads_step,
        [*xs, in_vmem(weight), wt],
        [(queries, BF16), (queries, F32), (states, F32), (levels, F32)],
        [pltpu.VMEM((chunks * ROWS, width), BF16), pltpu.VMEM((chunks, 8, ROWS), F32)],
    )


def project_tiles(tiles, seq, relative, weight, wt):
    width, cols = weight.shape
    heads = cols // 384
    heads_step = 2 if heads % 2 == 0 else 1
    weight = in_vmem(weight)
    queries, states = (1, heads * 128, ROWS), (1, heads, 128, 128)
    made, before = [], []
    for tile, xs in enumerate(tiles):
        made.append(
            vmem_call(
                keys_kernel(relative, seq, tile, heads),
                1,
                [*xs, weight, wt, *before],
                [
                    (states, F32),
                    ((heads, TILE, 128), BF16),
                    ((heads, 128, TILE), BF16),
                    ((heads, wt.shape[3], TILE), F32),
                    ((TILE, width), BF16),
                ],
                [pltpu.VMEM((1, 8, TILE), F32)],
            )
        )
        before = [in_vmem(made[-1][0])]
    pairs = [[in_vmem(call[i]) for call in made] for i in (4, 1, 2, 3)]
    q, near, scaled = vmem_call(
        queries_kernel(heads_step),
        heads // heads_step,
        [*pairs[0], weight, *pairs[1], *pairs[2], *pairs[3]],
        [(queries, BF16), (queries, F32), ((1, heads, wt.shape[3], ROWS), F32)],
        [pltpu.VMEM((ROWS, width), BF16)],
    )
    return q, near, made[-1][0], scaled


BEFORE = (1, 3, 0, 2)


def scaled_levels(q, wt_ref, c, head, levels):
    q16 = q.reshape(8, 16, ROWS)
    scaled = []
    for level in levels:
        row = jnp.broadcast_to(wt_ref[c, head, level : level + 1, :], (16, ROWS)).astype(BF16)
        scaled.append((q16 * row[None]).reshape(128, ROWS))
    return jnp.concatenate(scaled, axis=0)


def part_kernel(picks, half_heads):
    def body(*refs):
        qs, nears, states, wts = refs[0:4], refs[4:8], refs[8:12], refs[12:16]
        core_ref, mine_ref, other_ref = refs[16:19]
        out_ref = refs[-1]
        head = pl.program_id(0)
        rows = pl.ds(head * 128, 128)
        core = lax.axis_index("seq") % 2
        places = [place_of(r) for r in range(4)]
        st = [states[r][picks[r], head] for r in range(4)]
        buckets = [(core_ref[head].astype(F32) * core.astype(F32)).astype(BF16)]
        for j in range(mine_ref.shape[0]):
            at = head % half_heads
            buckets.append(jnp.where(head // half_heads == core, mine_ref[j, at], other_ref[j, at]))
        for r in range(4):
            place = places[r]
            level9 = st[BEFORE[r]] * (place % 2).astype(F32)
            upper = (place // 2).astype(F32)
            level10 = sum(
                [st[o] * (upper * (1 - places[o] // 2).astype(F32)) for o in range(4) if o != r]
            )
            mats = jnp.concatenate([level9.astype(BF16), level10.astype(BF16)] + buckets, axis=1)
            scaled = scaled_levels(
                qs[r][picks[r], rows, :], wts[r], picks[r], head, range(9, 11 + len(buckets))
            )
            out_ref[r, rows, :] = nears[r][picks[r], rows, :] + jnp.dot(
                mats, scaled, preferred_element_type=F32
            )

    return body


def finish_half(lengths_ref, refs, picks, half_heads, seq, first_level, half, done):
    qs, wts = refs[0:4], refs[4:8]
    part_ref, level_ref = refs[8:10]
    limit = lengths_ref[seq] - lax.axis_index("seq") * (4 * ROWS)
    levels = range(first_level, first_level + level_ref.shape[0])
    lane = lax.broadcasted_iota(jnp.int32, (1, ROWS), 1)
    for j in range(half_heads):
        head = half * half_heads + j
        rows = pl.ds(pl.multiple_of(head * 128, 128), 128)
        mats = jnp.concatenate([level_ref[i, j] for i in range(len(levels))], axis=1)
        for r in range(4):
            place = place_of(r)
            scaled = scaled_levels(qs[r][picks[r], rows, :], wts[r], picks[r], head, levels)
            acc = part_ref[r, rows, :] + jnp.dot(mats, scaled, preferred_element_type=F32)
            scale = lax.rsqrt(jnp.mean(acc * acc, 0, keepdims=True) + 1e-06)
            valid = place * ROWS + lane < limit
            acc = acc * jnp.where(valid, scale, 0.0)
            done(j, r, place, acc.astype(BF16).T)


def mine_kernel(picks, half_heads, seq, first_level):
    def body(lengths_ref, *refs):
        out_ref = refs[-1]

        def done(j, r, place, rows):
            out_ref[j, place] = rows

        core = lax.axis_index("seq") % 2
        finish_half(lengths_ref, refs, picks, half_heads, seq, first_level, core, done)

    return body


def last_kernel(picks, half_heads, seq, first_level):
    def body(lengths_ref, *refs):
        mine_ref = refs[10]
        out_ref, buf, sem, mine_sem = refs[-4:]
        core = lax.axis_index("seq") % 2
        copies = []

        def lanes(half, j):
            return pl.ds(pl.multiple_of((half * half_heads + j) * 128, 128), 128)

        for j in range(half_heads):
            copies.append(
                pltpu.make_async_copy(
                    mine_ref.at[j], out_ref.at[seq, :, :, lanes(core, j)], mine_sem.at[j]
                )
            )
            copies[-1].start()

        def done(j, r, place, rows):
            buf[j, r] = rows
            copies.append(
                pltpu.make_async_copy(
                    buf.at[j, r], out_ref.at[seq, place, :, lanes(1 - core, j)], sem.at[j, r]
                )
            )
            copies[-1].start()

        finish_half(lengths_ref, refs, picks, half_heads, seq, first_level, 1 - core, done)
        for copy in copies:
            copy.wait()

    return body


def far(lengths, chunks, found, seq, out_prev, seqs):
    core_bucket, x_levels, x_other, y_levels, y_other = found
    heads = core_bucket.shape[0]
    half_heads = heads // 2
    picks = [c for _, c in chunks]
    vmem = pl.BlockSpec(memory_space=pltpu.VMEM)
    columns = [[in_vmem(call[i]) for call, _ in chunks] for i in range(4)]
    args = columns[0] + columns[1] + columns[2] + columns[3] + [core_bucket, x_levels, x_other]
    part = pl.pallas_call(
        part_kernel(picks, half_heads),
        grid=(heads,),
        in_specs=[vmem] * len(args),
        out_specs=vmem,
        out_shape=pltpu.VMEM((4, heads * 128, ROWS), F32),
        compiler_params=pltpu.CompilerParams(vmem_limit_bytes=4 << 20),
        name="far_part",
    )(*args)
    first_level = 12 + x_levels.shape[0]
    smem = pl.BlockSpec(memory_space=pltpu.SMEM)
    half_shape = (half_heads, 4, ROWS, 128)
    args = [lengths] + columns[0] + columns[3] + [in_vmem(part), in_vmem(y_levels)]
    mine = pl.pallas_call(
        mine_kernel(picks, half_heads, seq, first_level),
        in_specs=[smem] + [vmem] * (len(args) - 1),
        out_specs=vmem,
        out_shape=pltpu.VMEM(half_shape, BF16),
        compiler_params=pltpu.CompilerParams(vmem_limit_bytes=4 << 20),
        name="far_mine",
    )(*args)
    args = args[:-1] + [in_vmem(y_other), in_vmem(mine)]
    in_specs = [smem] + [vmem] * (len(args) - 1)
    aliases = {}
    if out_prev is not None:
        in_specs.append(pl.BlockSpec(memory_space=pl.ANY))
        args.append(out_prev)
        aliases = {len(args) - 1: 0}
    return pl.pallas_call(
        last_kernel(picks, half_heads, seq, first_level),
        in_specs=in_specs,
        out_specs=pl.BlockSpec(memory_space=pl.ANY),
        out_shape=jax.ShapeDtypeStruct((seqs, 4, ROWS, heads * 128), BF16),
        scratch_shapes=[
            pltpu.VMEM(half_shape, BF16),
            pltpu.SemaphoreType.DMA((half_heads, 4)),
            pltpu.SemaphoreType.DMA((half_heads,)),
        ],
        input_output_aliases=aliases,
        compiler_params=pltpu.CompilerParams(vmem_limit_bytes=6 << 20),
        name="far_last",
    )(*args)


def small_call(body, outs, *args):
    return vmem_call(body, 1, [in_vmem(x) for x in args], outs, limit=4)


def seq_bit(j):
    return (lax.axis_index("seq") // (1 << j)) % 2


def total_kernel(own_ref, ab_ref, cd_ref, total_ref, sent_ref):
    total = own_ref[0] + ab_ref[0] + ab_ref[1] + cd_ref[0]
    total_ref[...] = total
    sent_ref[...] = total.astype(BF16)


def core_kernel(total_ref, received_ref, part_ref, sent_ref):
    half = part_ref.shape[0]
    heads = pl.ds(seq_bit(0) * half, half)
    part = total_ref[heads] + received_ref[heads].astype(F32)
    part_ref[...] = part
    sent_ref[...] = part.astype(BF16)


def stage_kernel(low, last):
    def body(part_ref, one_ref, two_ref, three_ref, mine_ref, *outs):
        one, two, three = [r[...].astype(F32) for r in (one_ref, two_ref, three_ref)]
        mine_ref[0] = (one * seq_bit(low).astype(F32)).astype(BF16)
        mine_ref[1] = ((two + three) * seq_bit(low + 1).astype(F32)).astype(BF16)
        if not last:
            next_ref, sent_ref = outs
            part = part_ref[...] + (one + (two + three))
            next_ref[...] = part
            sent_ref[...] = part.astype(BF16)

    return body


def exchange(own, ab, cd):
    size = lax.axis_size("seq")
    heads = own.shape[1]
    whole, half = (heads, 128, 128), (heads // 2, 128, 128)

    def swap(value, mask):
        return lax.ppermute(value, "seq", [(i, i ^ mask) for i in range(size)])

    total, sent = small_call(total_kernel, [(whole, F32), (whole, BF16)], own, ab, cd)
    core_bucket = swap(sent, 1)
    part, sent = small_call(core_kernel, [(half, F32), (half, BF16)], total, core_bucket)
    found = [core_bucket]
    for low in (1, 3):
        heard = [swap(sent, mask << low) for mask in (1, 2, 3)]
        outs = [((2,) + half, BF16), (half, F32), (half, BF16)]
        made = small_call(stage_kernel(low, low == 3), outs[: 1 if low == 3 else 3], part, *heard)
        found += [made[0], swap(made[0], 1)]
        if low == 1:
            part, sent = made[1:]
    return found


def on_device(tokens, norm_gain, projection, level_table, level_index, lengths):
    seqs, row_count, width = tokens.shape
    tables, heads, level_total = level_table.shape
    groups = lax.axis_size("head")
    half = row_count // 2
    up = [(i, (i + 1) % groups) for i in range(groups)]
    down = [(i, (i - 1) % groups) for i in range(groups)]

    got = []
    held = tokens
    for s in range(seqs):
        last = s + 1 == seqs
        if last:
            quarters = held[s].reshape(2, 2, half // 2, width)
            low, high = [quarters[:, i].reshape(1, half, width) for i in range(2)]
        else:
            low, high = held[s : s + 1, :half], held[s : s + 1, half:]
        a_low = lax.ppermute(low, "head", up)
        b_high = lax.ppermute(high, "head", down)
        a_high = lax.ppermute(high, "head", up)
        b_low = lax.ppermute(low, "head", down)
        if not last:
            held, a_low, b_high = lax.optimization_barrier((tokens, a_low, b_high))
            far_pieces = [lax.ppermute(a_low, "head", up), lax.ppermute(b_high, "head", down)]
        else:
            far_pieces = []
            for tile in range(2):
                rows = slice(tile * half // 2, (tile + 1) * half // 2)
                far_pieces.append(
                    [
                        lax.ppermute(a_low[:, rows], "head", up),
                        lax.ppermute(b_high[:, rows], "head", down),
                    ]
                )
        got.append(([a_low, a_high, b_low, b_high], far_pieces))

    level_rows = -(-level_total // 8) * 8
    onehot = (level_index[..., None] == jnp.arange(tables, dtype=jnp.int32)).astype(F32)
    table = jnp.pad(level_table, ((0, 0), (0, 0), (0, level_rows - level_total)))
    wt = jnp.einsum(
        "ghl,szrg->szhlr",
        table,
        onehot.reshape(seqs, groups, row_count, tables),
        precision=lax.Precision.HIGHEST,
    )

    weight = fold_gain(norm_gain, projection)

    own = []
    for s in range(seqs):
        own.append(project([tokens], s, [0], weight, wt, [(0, s, 0, row_count)]))
    parts = []
    for s in range(seqs):
        near_pieces, far_pieces = got[s]
        if s + 1 < seqs:
            blocks = [(i, 0, 0, half) for i in range(4)]
            cd = project(far_pieces, s, [3], weight, wt, blocks[:2])
        else:
            quarter = half // 2
            blocks = [
                (pair + i, 0, first, quarter)
                for pair in (0, 2)
                for first in (0, quarter)
                for i in range(2)
            ]
            cd = project_tiles(far_pieces, s, 3, weight, wt)
        ab = project(near_pieces, s, [1, 2], weight, wt, blocks)
        parts.append((ab, cd))

    out = None
    for s in range(seqs):
        ab, cd = parts[s]
        found = exchange(own[s][2], ab[2], cd[2])
        chunks = [(own[s], 0), (ab, 0), (ab, 1), (cd, 0)]
        out = far(lengths, chunks, found, s, out, seqs)
    return out.reshape(seqs, row_count * groups, heads * 128)


def solution(mesh):
    in_specs = (
        P(None, ("seq", "head"), None),
        P(),
        P(None, "head"),
        P(None, "head", None),
        P(None, "seq"),
        P(),
    )
    out_specs = P(None, "seq", "head")

    return jax.shard_map(on_device, mesh=mesh, in_specs=in_specs, out_specs=out_specs, check_vma=False)
```
